32 devices in a mesh: coarse: 8 (over y, x, core), fine: 4 (over z).
Axes of the slice: x: 2, y: 2, z: 4, core: 2. Of those that a mesh axis runs over, the one named last changes fastest.
Arguments:
- activations: bfloat16 [16384, 1280], P(('coarse', 'fine')), may hold values from -6 to 6
- targets: int32 [16384], P(('coarse', 'fine')), may hold values from 0 to 4
- inner_squeeze_weight: bfloat16 [1280, 640], replicated, may hold values from -0.15625 to 0.15625
- inner_filter_taps: bfloat16 [3, 640, 640], replicated, may hold values from -0.125 to 0.125
- inner_expand_weight: bfloat16 [640, 1280], replicated, may hold values from -0.25 to 0.25
- outer_squeeze_weight: bfloat16 [1280, 640], replicated, may hold values from -0.15625 to 0.15625
- outer_filter_taps: bfloat16 [3, 640, 640], replicated, may hold values from -0.125 to 0.125
- outer_expand_weight: bfloat16 [640, 1280], replicated, may hold values from -0.25 to 0.25
- decoder: bfloat16 [5, 1280], replicated, may hold values from -0.059814453 to 0.059814453
Outputs:
- input_gradient: bfloat16 [16384, 1280], P(('coarse', 'fine'))
- token_loss: float32 [16384], P(('coarse', 'fine'))
The draws below stay inside these ranges and needn't reach their ends.
All inputs are finite; a program needn't handle non-finite values.
Results may differ from the reference program's by a relative error of at most 0.015.
Values may be sent and summed in bfloat16 or wider, within the bound.
No kernel may reach another device: no remote copies, remote signals or barrier semaphores. Data moves between devices by JAX's collectives and lax.ppermute only.
A program may use at most 64 MiB of HBM per device.

```python
import math
import jax
import jax.numpy as jnp
from jax import lax

D = 1280
BOT = 640
VOCAB = 5
TAPS = 3
SEQ = 16384
INNER_DILATION = 1024
OUTER_DILATION = 8192


def set_ends(result, stream_key, least, top_value):
    longest = result.shape.index(max(result.shape))
    spots = []
    for shift in (0, 1):
        where = [jax.random.randint(jax.random.fold_in(stream_key, axis), (), 0, length) for axis, length in enumerate(result.shape)]
        where[longest] = (where[longest] + shift) % result.shape[longest]
        spots.append(tuple(where))
    return result.at[spots[0]].set(least).at[spots[1]].set(top_value)


def block_levels(own_key, extent, cuts, low, high):
    level = 1.0
    for dim, parts in cuts:
        steps = jax.random.uniform(jax.random.fold_in(jax.random.fold_in(own_key, 6), dim), (parts,), jnp.float32, low / len(cuts), high / len(cuts))
        level = level * jnp.repeat(jnp.exp(steps), extent[dim] // parts).reshape((-1,) + (1,) * (len(extent) - 1 - dim))
    return level


def noise(own_key, dims, scale, limit, shards=(), held_as=jnp.bfloat16):
    values = scale * jax.random.normal(own_key, dims, jnp.float32)
    if shards:
        values = values * block_levels(own_key, dims, shards, -0.22, 0.18)
    return jnp.clip(values, -limit, limit).astype(held_as)


def setup_inputs(seed: int = 0) -> dict:
    key_list = jax.random.split(jax.random.key(seed), 10)
    return {
        "activations": noise(key_list[0], (SEQ, D), 1.0, 6.0, ((0, 32),)),
        "targets": set_ends(jax.random.randint(key_list[1], (SEQ,), 0, VOCAB), jax.random.fold_in(key_list[1], 1), 0, VOCAB - 1).astype(jnp.int32),
        "inner_squeeze_weight": noise(key_list[2], (D, BOT), D ** -0.5, 0.15625),
        "inner_filter_taps": noise(key_list[3], (TAPS, BOT, BOT), (TAPS * BOT) ** -0.5, 0.125),
        "inner_expand_weight": noise(key_list[4], (BOT, D), BOT ** -0.5, 0.25),
        "outer_squeeze_weight": noise(key_list[5], (D, BOT), D ** -0.5, 0.15625),
        "outer_filter_taps": noise(key_list[6], (TAPS, BOT, BOT), (TAPS * BOT) ** -0.5, 0.125),
        "outer_expand_weight": noise(key_list[7], (BOT, D), BOT ** -0.5, 0.25),
        "decoder": jnp.clip(jax.random.uniform(key_list[8], (VOCAB, D), jnp.float32, -0.059814453, 0.059814453), -0.059814453, 0.059814453).astype(jnp.bfloat16),
    }


eps = 1e-05

def norm_rows(values):
    average = lax.optimization_barrier(jnp.mean(values, axis=-1, keepdims=True))
    centred = values - average
    factor = lax.rsqrt(lax.optimization_barrier(jnp.mean(centred * centred, axis=-1, keepdims=True)) + eps)
    return (centred * factor, factor)

def norm_back(normal, factor, upward):
    first_term = upward - lax.optimization_barrier(jnp.mean(upward, axis=-1, keepdims=True))
    return (first_term - normal * lax.optimization_barrier(jnp.mean(upward * normal, axis=-1, keepdims=True))) * factor

def gelu_exact(inputs):
    return 0.5 * inputs * (1.0 + lax.erf(inputs * (1.0 / math.sqrt(2.0))))

def gelu_slope(inputs):
    return 0.5 * (1.0 + lax.erf(inputs * (1.0 / math.sqrt(2.0)))) + inputs * jnp.exp(-0.5 * inputs * inputs) * (1.0 / math.sqrt(2.0 * math.pi))

def product(leading, trailing):
    return jnp.dot(leading, trailing, preferred_element_type=jnp.float32)

def product_t(leading, trailing):
    return lax.dot_general(leading, trailing, (((1,), (1,)), ((), ())), preferred_element_type=jnp.float32)

def residual_block_forward(block_in, squeeze, taps, expand, dilation):
    normal_in, _ = norm_rows(block_in.astype(jnp.float32))
    entry_act = gelu_exact(normal_in).astype(jnp.bfloat16)
    squeezed = product(entry_act, squeeze)
    normal_mid, _ = norm_rows(squeezed)
    middle = gelu_exact(normal_mid).astype(jnp.bfloat16)
    conv_sum = product(jnp.roll(middle, dilation, 0), taps[0]) + product(middle, taps[1]) + product(jnp.roll(middle, -dilation, 0), taps[2])
    normal_conv, _ = norm_rows(conv_sum)
    closing = gelu_exact(normal_conv).astype(jnp.bfloat16)
    block_out = (block_in.astype(jnp.float32) + product(closing, expand)).astype(jnp.bfloat16)
    return (block_out, squeezed, conv_sum)

def residual_block_backward(block_in, squeezed, conv_sum, squeeze, taps, expand, dilation, gradient_result):
    dclosing = product_t(gradient_result.astype(jnp.bfloat16), expand)
    normal_conv, factor_conv = norm_rows(conv_sum)
    dconv = norm_back(normal_conv, factor_conv, gelu_slope(normal_conv) * dclosing).astype(jnp.bfloat16)
    dmiddle = product_t(jnp.roll(dconv, -dilation, 0), taps[0]) + product_t(dconv, taps[1]) + product_t(jnp.roll(dconv, dilation, 0), taps[2])
    normal_mid, factor_mid = norm_rows(squeezed)
    dsqueezed = norm_back(normal_mid, factor_mid, gelu_slope(normal_mid) * dmiddle).astype(jnp.bfloat16)
    dentry = product_t(dsqueezed, squeeze)
    normal_in, factor_in = norm_rows(block_in.astype(jnp.float32))
    return gradient_result + norm_back(normal_in, factor_in, gelu_slope(normal_in) * dentry)

def reference(activations, targets, inner_squeeze_weight, inner_filter_taps, inner_expand_weight, outer_squeeze_weight, outer_filter_taps, outer_expand_weight, decoder):
    outer_block_input, inner_bottleneck_rows, inner_convolved = residual_block_forward(activations, inner_squeeze_weight, inner_filter_taps, inner_expand_weight, INNER_DILATION)
    final_output, outer_bottleneck_rows, outer_convolved = residual_block_forward(outer_block_input, outer_squeeze_weight, outer_filter_taps, outer_expand_weight, OUTER_DILATION)
    normal_final, factor_final = norm_rows(final_output.astype(jnp.float32))
    normed = normal_final.astype(jnp.bfloat16)
    logits = product_t(normed, decoder)
    exponent = jnp.exp(logits)
    totals = lax.optimization_barrier(jnp.sum(exponent, axis=-1, keepdims=True))
    onehot = (targets[:, None] == jnp.arange(VOCAB, dtype=jnp.int32)[None, :]).astype(jnp.float32)
    token_loss = jnp.log(totals[:, 0]) - lax.optimization_barrier(jnp.sum(logits * onehot, axis=-1))
    dlogits = (32.0 * (exponent / totals - onehot)).astype(jnp.bfloat16)
    gradient_result = norm_back(normal_final, factor_final, product(dlogits, decoder))
    gradient_result = residual_block_backward(outer_block_input, outer_bottleneck_rows, outer_convolved, outer_squeeze_weight, outer_filter_taps, outer_expand_weight, OUTER_DILATION, gradient_result)
    gradient_result = residual_block_backward(activations, inner_bottleneck_rows, inner_convolved, inner_squeeze_weight, inner_filter_taps, inner_expand_weight, INNER_DILATION, gradient_result)
    return (gradient_result.astype(jnp.bfloat16), token_loss)
```

```python
import functools
import math

import jax
import jax.numpy as jnp
from jax import lax
from jax.experimental import pallas as pl
from jax.experimental.pallas import tpu as pltpu
from jax.sharding import PartitionSpec as P

COARSE_HOP = 4
FINE_HOP = 2
LANES = 128
CHUNKS = 1
BLOCK = 128


eps = 1e-05


def from_behind(value, axis, steps):
    count = lax.axis_size(axis)
    pairs = [(source, (source + steps) % count) for source in range(count)]
    return lax.ppermute(value, axis, pairs)


def norm_rows(values):
    average = jnp.mean(values, axis=-1, keepdims=True)
    centred = values - average
    factor = lax.rsqrt(jnp.mean(centred * centred, axis=-1, keepdims=True) + eps)
    return (centred * factor, factor)


def norm_back(normal, factor, upward):
    first_term = upward - jnp.mean(upward, axis=-1, keepdims=True)
    return (first_term - normal * jnp.mean(upward * normal, axis=-1, keepdims=True)) * factor


def gelu_exact(inputs):
    return 0.5 * inputs * (1.0 + lax.erf(inputs * (1.0 / math.sqrt(2.0))))


def gelu_slope(inputs):
    return 0.5 * (1.0 + lax.erf(inputs * (1.0 / math.sqrt(2.0)))) + inputs * jnp.exp(
        -0.5 * inputs * inputs
    ) * (1.0 / math.sqrt(2.0 * math.pi))


def product(leading, trailing):
    return jnp.dot(leading, trailing, preferred_element_type=jnp.float32)


def product_t(leading, trailing):
    return lax.dot_general(
        leading, trailing, (((1,), (1,)), ((), ())), preferred_element_type=jnp.float32
    )


def inner_pair(shard_rows):
    near_behind = from_behind(shard_rows, "fine", 2)
    near_ahead = from_behind(shard_rows, "fine", -2)
    far_behind = from_behind(near_behind, "coarse", 1)
    far_ahead = from_behind(near_ahead, "coarse", -1)
    fine_index = lax.axis_index("fine")
    fine_count = lax.axis_size("fine")
    behind_rows = jnp.where(fine_index < 2, far_behind, near_behind)
    ahead_rows = jnp.where(fine_index >= fine_count - 2, far_ahead, near_ahead)
    return (behind_rows, ahead_rows)


def outer_pair(shard_rows):
    behind_rows = from_behind(shard_rows, "coarse", COARSE_HOP)
    ahead_rows = from_behind(shard_rows, "coarse", -COARSE_HOP)
    return (behind_rows, ahead_rows)


def residual_block_forward(block_in, squeeze, taps, expand, neighbours):
    normal_in, _ = norm_rows(block_in.astype(jnp.float32))
    entry_act = gelu_exact(normal_in).astype(jnp.bfloat16)
    squeezed = product(entry_act, squeeze)
    normal_mid, _ = norm_rows(squeezed)
    middle = gelu_exact(normal_mid).astype(jnp.bfloat16)
    behind_rows, ahead_rows = neighbours(middle)
    conv_sum = (
        product(behind_rows, taps[0]) + product(middle, taps[1]) + product(ahead_rows, taps[2])
    )
    normal_conv, _ = norm_rows(conv_sum)
    closing = gelu_exact(normal_conv).astype(jnp.bfloat16)
    block_out = (block_in.astype(jnp.float32) + product(closing, expand)).astype(jnp.bfloat16)
    return (block_out, squeezed, conv_sum)


def residual_block_backward(
    block_in, squeezed, conv_sum, squeeze, taps, expand, neighbours, gradient_result
):
    dclosing = product_t(gradient_result.astype(jnp.bfloat16), expand)
    normal_conv, factor_conv = norm_rows(conv_sum)
    dconv = norm_back(normal_conv, factor_conv, gelu_slope(normal_conv) * dclosing).astype(
        jnp.bfloat16
    )
    behind_rows, ahead_rows = neighbours(dconv)
    dmiddle = (
        product_t(ahead_rows, taps[0]) + product_t(dconv, taps[1]) + product_t(behind_rows, taps[2])
    )
    normal_mid, factor_mid = norm_rows(squeezed)
    dsqueezed = norm_back(normal_mid, factor_mid, gelu_slope(normal_mid) * dmiddle).astype(
        jnp.bfloat16
    )
    dentry = product_t(dsqueezed, squeeze)
    normal_in, factor_in = norm_rows(block_in.astype(jnp.float32))
    return gradient_result + norm_back(normal_in, factor_in, gelu_slope(normal_in) * dentry)


def on_device(
    activations,
    targets,
    inner_squeeze_weight,
    inner_filter_taps,
    inner_expand_weight,
    outer_squeeze_weight,
    outer_filter_taps,
    outer_expand_weight,
    decoder,
):
    outer_block_input, inner_bottleneck_rows, inner_convolved = residual_block_forward(
        activations, inner_squeeze_weight, inner_filter_taps, inner_expand_weight, inner_pair
    )
    final_output, outer_bottleneck_rows, outer_convolved = residual_block_forward(
        outer_block_input, outer_squeeze_weight, outer_filter_taps, outer_expand_weight, outer_pair
    )
    normal_final, factor_final = norm_rows(final_output.astype(jnp.float32))
    normed = normal_final.astype(jnp.bfloat16)
    logits = product_t(normed, decoder)
    exponent = jnp.exp(logits)
    totals = jnp.sum(exponent, axis=-1, keepdims=True)
    classes = jnp.arange(decoder.shape[0], dtype=jnp.int32)
    onehot = (targets[:, None] == classes[None, :]).astype(jnp.float32)
    token_loss = jnp.log(totals[:, 0]) - jnp.sum(logits * onehot, axis=-1)
    dlogits = (32.0 * (exponent / totals - onehot)).astype(jnp.bfloat16)
    gradient_result = norm_back(normal_final, factor_final, product(dlogits, decoder))
    gradient_result = residual_block_backward(
        outer_block_input,
        outer_bottleneck_rows,
        outer_convolved,
        outer_squeeze_weight,
        outer_filter_taps,
        outer_expand_weight,
        outer_pair,
        gradient_result,
    )
    gradient_result = residual_block_backward(
        activations,
        inner_bottleneck_rows,
        inner_convolved,
        inner_squeeze_weight,
        inner_filter_taps,
        inner_expand_weight,
        inner_pair,
        gradient_result,
    )
    return (gradient_result.astype(jnp.bfloat16), token_loss)


BF = jnp.bfloat16
F32 = jnp.float32


def activate(values, normal_ref, slope_ref, factor_ref, rows):
    normal, factor = norm_rows(values)
    half = 0.5 * (1.0 + lax.erf(normal * (1.0 / math.sqrt(2.0))))
    bell = jnp.exp(-0.5 * normal * normal) * (1.0 / math.sqrt(2.0 * math.pi))
    normal_ref[rows, :] = normal
    slope_ref[rows, :] = half + normal * bell
    factor_ref[rows, :] = jnp.broadcast_to(factor, (factor.shape[0], LANES))
    return (normal * half).astype(BF)


def back(upward, normal_ref, slope_ref, factor_ref, rows):
    factor = factor_ref[rows, :][:, :1]
    return norm_back(normal_ref[rows, :], factor, slope_ref[rows, :] * upward)


def chain_kernel(
    near, far, classes, block,
    x_ref, onehot_ref, ws_in, wt_in, we_in, ws_out, wt_out, we_out, dec_ref,
    grad_ref, loss_ref,
    mid_a, mid_b, outer_in, carried,
    n_in_a, s_in_a, f_in_a, n_mid_a, s_mid_a, f_mid_a, n_con_a, s_con_a, f_con_a,
    n_in_b, s_in_b, f_in_b, n_mid_b, s_mid_b, f_mid_b, n_con_b, s_con_b, f_con_b,
):
    total = x_ref.shape[0]
    steps = total // block

    def each(body):
        def run(step, carry):
            body(pl.multiple_of(step * block, block))
            return carry

        lax.fori_loop(0, steps, run, 0)

    def wrap(ref):
        ref[pl.ds(0, near), :] = ref[pl.ds(total, near), :]
        ref[pl.ds(total + near, near), :] = ref[pl.ds(near, near), :]

    def near_rows(ref, start, shift):
        return ref[pl.ds(pl.multiple_of(start + near + shift, near), block), :]

    def far_rows(ref, start, shift):
        return ref[pl.ds(pl.multiple_of(lax.rem(start + shift, total), block), block), :]

    def enter(start):
        rows = pl.ds(start, block)
        entry = activate(x_ref[rows, :].astype(F32), n_in_a, s_in_a, f_in_a, rows)
        squeezed = product(entry, ws_in[...])
        middle = activate(squeezed, n_mid_a, s_mid_a, f_mid_a, rows)
        mid_a[pl.ds(pl.multiple_of(start + near, near), block), :] = middle

    each(enter)
    wrap(mid_a)

    def inner(start):
        rows = pl.ds(start, block)
        conv = (
            product(near_rows(mid_a, start, -near), wt_in[0])
            + product(near_rows(mid_a, start, 0), wt_in[1])
            + product(near_rows(mid_a, start, near), wt_in[2])
        )
        closing = activate(conv, n_con_a, s_con_a, f_con_a, rows)
        following = (x_ref[rows, :].astype(F32) + product(closing, we_in[...])).astype(BF)
        outer_in[rows, :] = following
        entry = activate(following.astype(F32), n_in_b, s_in_b, f_in_b, rows)
        squeezed = product(entry, ws_out[...])
        mid_b[rows, :] = activate(squeezed, n_mid_b, s_mid_b, f_mid_b, rows)

    each(inner)

    def outer(start):
        rows = pl.ds(start, block)
        conv = (
            product(far_rows(mid_b, start, total - far), wt_out[0])
            + product(mid_b[rows, :], wt_out[1])
            + product(far_rows(mid_b, start, far), wt_out[2])
        )
        closing = activate(conv, n_con_b, s_con_b, f_con_b, rows)
        final = (outer_in[rows, :].astype(F32) + product(closing, we_out[...])).astype(BF)
        normal, factor = norm_rows(final.astype(F32))
        logits = product_t(normal.astype(BF), dec_ref[...])
        lane = lax.broadcasted_iota(jnp.int32, logits.shape, 1)
        exponent = jnp.where(lane < classes, jnp.exp(logits), 0.0)
        totals = jnp.sum(exponent, axis=-1, keepdims=True)
        onehot = onehot_ref[rows, :].astype(F32)
        loss = jnp.log(totals) - jnp.sum(logits * onehot, axis=-1, keepdims=True)
        loss = jnp.broadcast_to(loss, (block, LANES))
        for part in range(block // LANES):
            flat = jnp.transpose(loss[part * LANES : (part + 1) * LANES, :])
            loss_ref[pl.ds(start // LANES + part, 1), :] = flat[:1, :]
        dlogits = (32.0 * (exponent / totals - onehot)).astype(BF)
        upward = norm_back(normal, factor, product(dlogits, dec_ref[...]))
        carried[rows, :] = upward
        dclosing = product_t(upward.astype(BF), we_out[...])
        mid_a[rows, :] = back(dclosing, n_con_b, s_con_b, f_con_b, rows).astype(BF)

    each(outer)

    def outer_back(start):
        rows = pl.ds(start, block)
        dmiddle = (
            product_t(far_rows(mid_a, start, far), wt_out[0])
            + product_t(mid_a[rows, :], wt_out[1])
            + product_t(far_rows(mid_a, start, total - far), wt_out[2])
        )
        dsqueezed = back(dmiddle, n_mid_b, s_mid_b, f_mid_b, rows).astype(BF)
        dentry = product_t(dsqueezed, ws_out[...])
        upward = carried[rows, :] + back(dentry, n_in_b, s_in_b, f_in_b, rows)
        carried[rows, :] = upward
        dclosing = product_t(upward.astype(BF), we_in[...])
        mid_b[pl.ds(pl.multiple_of(start + near, near), block), :] = back(
            dclosing, n_con_a, s_con_a, f_con_a, rows
        ).astype(BF)

    each(outer_back)
    wrap(mid_b)

    def inner_back(start):
        rows = pl.ds(start, block)
        dmiddle = (
            product_t(near_rows(mid_b, start, near), wt_in[0])
            + product_t(near_rows(mid_b, start, 0), wt_in[1])
            + product_t(near_rows(mid_b, start, -near), wt_in[2])
        )
        dsqueezed = back(dmiddle, n_mid_a, s_mid_a, f_mid_a, rows).astype(BF)
        dentry = product_t(dsqueezed, ws_in[...])
        upward = carried[rows, :] + back(dentry, n_in_a, s_in_a, f_in_a, rows)
        grad_ref[rows, :] = upward.astype(BF)

    each(inner_back)


def run_chains(rows, onehot, weights, near, far, classes, block):
    count, width = rows.shape
    bottleneck = weights[0].shape[1]
    padded = count + 2 * near

    def kept(size):
        return [
            pltpu.VMEM((count, size), F32),
            pltpu.VMEM((count, size), F32),
            pltpu.VMEM((count, LANES), F32),
        ]

    one_block = kept(width) + kept(bottleneck) + kept(bottleneck)
    return pl.pallas_call(
        functools.partial(chain_kernel, near, far, classes, block),
        out_shape=(
            jax.ShapeDtypeStruct((count, width), BF),
            jax.ShapeDtypeStruct((count // LANES, LANES), F32),
        ),
        in_specs=[pl.BlockSpec(memory_space=pltpu.VMEM)] * (2 + len(weights)),
        out_specs=(
            pl.BlockSpec(memory_space=pltpu.VMEM),
            pl.BlockSpec(memory_space=pltpu.VMEM),
        ),
        scratch_shapes=[
            pltpu.VMEM((padded, bottleneck), BF),
            pltpu.VMEM((padded, bottleneck), BF),
            pltpu.VMEM((count, width), BF),
            pltpu.VMEM((count, width), F32),
        ]
        + one_block
        + one_block,
        compiler_params=pltpu.CompilerParams(vmem_limit_bytes=60 * 1024 * 1024),
        cost_estimate=pl.CostEstimate(
            flops=count * 36 * width * bottleneck, bytes_accessed=24 << 20, transcendentals=0
        ),
    )(rows, onehot, *weights)


def on_device_chains(chunks, block, activations, targets, *weights):
    axes = ("coarse", "fine")
    devices = lax.axis_size(axes)
    rows, width = activations.shape
    decoder = weights[-1]
    classes = decoder.shape[0]
    padded = jnp.pad(decoder, ((0, LANES - classes), (0, 0)))
    weights = weights[:-1] + (padded,)
    part = rows // chunks
    each = part // devices
    near = FINE_HOP * each
    far = COARSE_HOP * lax.axis_size("fine") * each

    def spread(values):
        shaped = values.reshape((devices, each) + values.shape[1:])
        moved = lax.all_to_all(shaped, axes, 0, 0, tiled=True)
        return moved.reshape(values.shape)

    grads, losses = [], []
    lane = jnp.arange(LANES, dtype=jnp.int32)
    for chunk in range(chunks):
        piece = slice(chunk * part, (chunk + 1) * part)
        there = spread(activations[piece])
        onehot = (spread(targets[piece])[:, None] == lane[None, :]).astype(BF)
        grad, loss = run_chains(there, onehot, weights, near, far, classes, block)
        grads.append(spread(grad))
        losses.append(spread(loss.reshape(part)))
    return (jnp.concatenate(grads), jnp.concatenate(losses))


def chains_fit(mesh, rows, chunks, block):
    devices = mesh.shape["coarse"] * mesh.shape["fine"]
    part = rows // chunks
    if rows % chunks or part % devices or part % block or block % LANES:
        return False
    each = part // devices
    far = COARSE_HOP * mesh.shape["fine"] * each
    return (FINE_HOP * each) % 16 == 0 and block % (FINE_HOP * each) == 0 and far % block == 0


def solution(mesh):
    in_specs = (
        P(("coarse", "fine"), None),
        P(("coarse", "fine")),
        P(),
        P(),
        P(),
        P(),
        P(),
        P(),
        P(),
    )
    out_specs = (P(("coarse", "fine"), None), P(("coarse", "fine")))

    def step(activations, *others):
        rows = activations.shape[0] // mesh.size
        body = on_device
        if chains_fit(mesh, rows, CHUNKS, BLOCK):
            body = functools.partial(on_device_chains, CHUNKS, BLOCK)
        return jax.shard_map(
            body, mesh=mesh, in_specs=in_specs, out_specs=out_specs, check_vma=False
        )(activations, *others)

    return step
```

```python
import functools
import math

import jax
import jax.numpy as jnp
from jax import lax
from jax.experimental import pallas as pl
from jax.experimental.pallas import tpu as pltpu
from jax.sharding import PartitionSpec as P


COARSE_HOP = 4
FINE_HOP = 2
LANES = 128
PIECES = 3
CHUNKS = 2
BLOCK = 256


eps = 1e-05


def from_behind(value, axis, steps):
    count = lax.axis_size(axis)
    pairs = [(source, (source + steps) % count) for source in range(count)]
    return lax.ppermute(value, axis, pairs)


def norm_rows(values):
    average = jnp.mean(values, axis=-1, keepdims=True)
    centred = values - average
    factor = lax.rsqrt(jnp.mean(centred * centred, axis=-1, keepdims=True) + eps)
    return (centred * factor, factor)


def norm_back(normal, factor, upward):
    first_term = upward - jnp.mean(upward, axis=-1, keepdims=True)
    return (first_term - normal * jnp.mean(upward * normal, axis=-1, keepdims=True)) * factor


def gelu_exact(inputs):
    return 0.5 * inputs * (1.0 + lax.erf(inputs * (1.0 / math.sqrt(2.0))))


def gelu_slope(inputs):
    return 0.5 * (1.0 + lax.erf(inputs * (1.0 / math.sqrt(2.0)))) + inputs * jnp.exp(
        -0.5 * inputs * inputs
    ) * (1.0 / math.sqrt(2.0 * math.pi))


def product(leading, trailing):
    return jnp.dot(leading, trailing, preferred_element_type=jnp.float32)


def product_t(leading, trailing):
    return lax.dot_general(
        leading, trailing, (((1,), (1,)), ((), ())), preferred_element_type=jnp.float32
    )


def inner_pair(shard_rows):
    near_behind = from_behind(shard_rows, "fine", 2)
    near_ahead = from_behind(shard_rows, "fine", -2)
    far_behind = from_behind(near_behind, "coarse", 1)
    far_ahead = from_behind(near_ahead, "coarse", -1)
    fine_index = lax.axis_index("fine")
    fine_count = lax.axis_size("fine")
    behind_rows = jnp.where(fine_index < 2, far_behind, near_behind)
    ahead_rows = jnp.where(fine_index >= fine_count - 2, far_ahead, near_ahead)
    return (behind_rows, ahead_rows)


def outer_pair(shard_rows):
    behind_rows = from_behind(shard_rows, "coarse", COARSE_HOP)
    ahead_rows = from_behind(shard_rows, "coarse", -COARSE_HOP)
    return (behind_rows, ahead_rows)


def residual_block_forward(block_in, squeeze, taps, expand, neighbours):
    normal_in, _ = norm_rows(block_in.astype(jnp.float32))
    entry_act = gelu_exact(normal_in).astype(jnp.bfloat16)
    squeezed = product(entry_act, squeeze)
    normal_mid, _ = norm_rows(squeezed)
    middle = gelu_exact(normal_mid).astype(jnp.bfloat16)
    behind_rows, ahead_rows = neighbours(middle)
    conv_sum = (
        product(behind_rows, taps[0]) + product(middle, taps[1]) + product(ahead_rows, taps[2])
    )
    normal_conv, _ = norm_rows(conv_sum)
    closing = gelu_exact(normal_conv).astype(jnp.bfloat16)
    block_out = (block_in.astype(jnp.float32) + product(closing, expand)).astype(jnp.bfloat16)
    return (block_out, squeezed, conv_sum)


def residual_block_backward(
    block_in, squeezed, conv_sum, squeeze, taps, expand, neighbours, gradient_result
):
    dclosing = product_t(gradient_result.astype(jnp.bfloat16), expand)
    normal_conv, factor_conv = norm_rows(conv_sum)
    dconv = norm_back(normal_conv, factor_conv, gelu_slope(normal_conv) * dclosing).astype(
        jnp.bfloat16
    )
    behind_rows, ahead_rows = neighbours(dconv)
    dmiddle = (
        product_t(ahead_rows, taps[0]) + product_t(dconv, taps[1]) + product_t(behind_rows, taps[2])
    )
    normal_mid, factor_mid = norm_rows(squeezed)
    dsqueezed = norm_back(normal_mid, factor_mid, gelu_slope(normal_mid) * dmiddle).astype(
        jnp.bfloat16
    )
    dentry = product_t(dsqueezed, squeeze)
    normal_in, factor_in = norm_rows(block_in.astype(jnp.float32))
    return gradient_result + norm_back(normal_in, factor_in, gelu_slope(normal_in) * dentry)


def on_device(
    activations,
    targets,
    inner_squeeze_weight,
    inner_filter_taps,
    inner_expand_weight,
    outer_squeeze_weight,
    outer_filter_taps,
    outer_expand_weight,
    decoder,
):
    outer_block_input, inner_bottleneck_rows, inner_convolved = residual_block_forward(
        activations, inner_squeeze_weight, inner_filter_taps, inner_expand_weight, inner_pair
    )
    final_output, outer_bottleneck_rows, outer_convolved = residual_block_forward(
        outer_block_input, outer_squeeze_weight, outer_filter_taps, outer_expand_weight, outer_pair
    )
    normal_final, factor_final = norm_rows(final_output.astype(jnp.float32))
    normed = normal_final.astype(jnp.bfloat16)
    logits = product_t(normed, decoder)
    exponent = jnp.exp(logits)
    totals = jnp.sum(exponent, axis=-1, keepdims=True)
    classes = jnp.arange(decoder.shape[0], dtype=jnp.int32)
    onehot = (targets[:, None] == classes[None, :]).astype(jnp.float32)
    token_loss = jnp.log(totals[:, 0]) - jnp.sum(logits * onehot, axis=-1)
    dlogits = (32.0 * (exponent / totals - onehot)).astype(jnp.bfloat16)
    gradient_result = norm_back(normal_final, factor_final, product(dlogits, decoder))
    gradient_result = residual_block_backward(
        outer_block_input,
        outer_bottleneck_rows,
        outer_convolved,
        outer_squeeze_weight,
        outer_filter_taps,
        outer_expand_weight,
        outer_pair,
        gradient_result,
    )
    gradient_result = residual_block_backward(
        activations,
        inner_bottleneck_rows,
        inner_convolved,
        inner_squeeze_weight,
        inner_filter_taps,
        inner_expand_weight,
        inner_pair,
        gradient_result,
    )
    return (gradient_result.astype(jnp.bfloat16), token_loss)


BF = jnp.bfloat16
F32 = jnp.float32


def activate(values, normal_ref, slope_ref, factor_ref, rows):
    normal, factor = norm_rows(values)
    half = 0.5 * (1.0 + lax.erf(normal * (1.0 / math.sqrt(2.0))))
    bell = jnp.exp(-0.5 * normal * normal) * (1.0 / math.sqrt(2.0 * math.pi))
    normal_ref[rows, :] = normal
    slope_ref[rows, :] = half + normal * bell
    factor_ref[rows, :] = jnp.broadcast_to(factor, (factor.shape[0], LANES))
    return (normal * half).astype(BF)


def back(upward, normal_ref, slope_ref, factor_ref, rows):
    factor = factor_ref[rows, :][:, :1]
    return norm_back(normal_ref[rows, :], factor, slope_ref[rows, :] * upward)


def chain_kernel(
    near, far, classes, block, chunk,
    x_ref, target_ref, before_ref, ws_in, wt_in, we_in, ws_out, wt_out, we_out, dec_ref,
    grad_ref, loss_ref,
    mid_a, mid_b, outer_in, carried,
    n_in_a, s_in_a, f_in_a, n_mid_a, s_mid_a, f_mid_a, n_con_a, s_con_a, f_con_a,
    n_in_b, s_in_b, f_in_b, n_mid_b, s_mid_b, f_mid_b, n_con_b, s_con_b, f_con_b,
):
    total = x_ref.shape[0]
    steps = total // block

    def each(body):
        def run(step, carry):
            body(pl.multiple_of(step * block, block))
            return carry

        if steps == 1:
            body(0)
        else:
            lax.fori_loop(0, steps, run, 0)

    def wrap(ref):
        ref[pl.ds(0, near), :] = ref[pl.ds(total, near), :]
        ref[pl.ds(total + near, near), :] = ref[pl.ds(near, near), :]

    def aligned(start, step):
        return start if isinstance(start, int) else pl.multiple_of(start, step)

    def near_rows(ref, start, shift):
        return ref[pl.ds(aligned(start + near + shift, near), block), :]

    def far_rows(ref, start, shift):
        if steps == 1:
            return jnp.concatenate([ref[shift:total, :], ref[:shift, :]])
        return ref[pl.ds(aligned(lax.rem(start + shift, total), block), block), :]

    def enter(start):
        rows = pl.ds(start, block)
        entry = activate(x_ref[rows, :].astype(F32), n_in_a, s_in_a, f_in_a, rows)
        squeezed = product(entry, ws_in[...])
        middle = activate(squeezed, n_mid_a, s_mid_a, f_mid_a, rows)
        mid_a[pl.ds(aligned(start + near, near), block), :] = middle

    each(enter)
    wrap(mid_a)

    def inner(start):
        rows = pl.ds(start, block)
        conv = (
            product(near_rows(mid_a, start, -near), wt_in[0])
            + product(near_rows(mid_a, start, 0), wt_in[1])
            + product(near_rows(mid_a, start, near), wt_in[2])
        )
        closing = activate(conv, n_con_a, s_con_a, f_con_a, rows)
        following = (x_ref[rows, :].astype(F32) + product(closing, we_in[...])).astype(BF)
        outer_in[rows, :] = following
        entry = activate(following.astype(F32), n_in_b, s_in_b, f_in_b, rows)
        squeezed = product(entry, ws_out[...])
        mid_b[rows, :] = activate(squeezed, n_mid_b, s_mid_b, f_mid_b, rows)

    each(inner)

    def outer(start):
        rows = pl.ds(start, block)
        conv = (
            product(far_rows(mid_b, start, total - far), wt_out[0])
            + product(mid_b[rows, :], wt_out[1])
            + product(far_rows(mid_b, start, far), wt_out[2])
        )
        closing = activate(conv, n_con_b, s_con_b, f_con_b, rows)
        final = (outer_in[rows, :].astype(F32) + product(closing, we_out[...])).astype(BF)
        normal, factor = norm_rows(final.astype(F32))
        logits = product_t(normal.astype(BF), dec_ref[...])
        lane = lax.broadcasted_iota(jnp.int32, logits.shape, 1)
        exponent = jnp.where(lane < classes, jnp.exp(logits), 0.0)
        totals = jnp.sum(exponent, axis=-1, keepdims=True)
        target = target_ref[rows, :].astype(F32)[:, chunk : chunk + 1]
        onehot = jnp.where(lane.astype(F32) == target, 1.0, 0.0)
        loss = jnp.log(totals) - jnp.sum(logits * onehot, axis=-1, keepdims=True)
        pieces = before_ref[rows, :].astype(F32)
        for part in range(PIECES):
            piece = loss.astype(BF).astype(F32)
            pieces = jnp.where(lane == chunk * PIECES + part, piece, pieces)
            loss = loss - piece
        loss_ref[rows, :] = pieces.astype(BF)
        dlogits = (32.0 * (exponent / totals - onehot)).astype(BF)
        upward = norm_back(normal, factor, product(dlogits, dec_ref[...]))
        carried[rows, :] = upward
        dclosing = product_t(upward.astype(BF), we_out[...])
        mid_a[rows, :] = back(dclosing, n_con_b, s_con_b, f_con_b, rows).astype(BF)

    each(outer)

    def outer_back(start):
        rows = pl.ds(start, block)
        dmiddle = (
            product_t(far_rows(mid_a, start, far), wt_out[0])
            + product_t(mid_a[rows, :], wt_out[1])
            + product_t(far_rows(mid_a, start, total - far), wt_out[2])
        )
        dsqueezed = back(dmiddle, n_mid_b, s_mid_b, f_mid_b, rows).astype(BF)
        dentry = product_t(dsqueezed, ws_out[...])
        upward = carried[rows, :] + back(dentry, n_in_b, s_in_b, f_in_b, rows)
        carried[rows, :] = upward
        dclosing = product_t(upward.astype(BF), we_in[...])
        mid_b[pl.ds(aligned(start + near, near), block), :] = back(
            dclosing, n_con_a, s_con_a, f_con_a, rows
        ).astype(BF)

    each(outer_back)
    wrap(mid_b)

    def inner_back(start):
        rows = pl.ds(start, block)
        dmiddle = (
            product_t(near_rows(mid_b, start, near), wt_in[0])
            + product_t(near_rows(mid_b, start, 0), wt_in[1])
            + product_t(near_rows(mid_b, start, -near), wt_in[2])
        )
        dsqueezed = back(dmiddle, n_mid_a, s_mid_a, f_mid_a, rows).astype(BF)
        dentry = product_t(dsqueezed, ws_in[...])
        upward = carried[rows, :] + back(dentry, n_in_a, s_in_a, f_in_a, rows)
        grad_ref[rows, :] = upward.astype(BF)

    each(inner_back)


def run_chains(rows, targets, before, weights, near, far, classes, block, chunk):
    count = rows.shape[0]
    width = weights[0].shape[0]
    bottleneck = weights[0].shape[1]
    padded = count + 2 * near

    def kept(size):
        return [
            pltpu.VMEM((count, size), F32),
            pltpu.VMEM((count, size), F32),
            pltpu.VMEM((count, LANES), F32),
        ]

    one_block = kept(width) + kept(bottleneck) + kept(bottleneck)
    return pl.pallas_call(
        functools.partial(chain_kernel, near, far, classes, block, chunk),
        out_shape=(
            jax.ShapeDtypeStruct((count, width), BF),
            jax.ShapeDtypeStruct((count, LANES), BF),
        ),
        in_specs=[pl.BlockSpec(memory_space=pltpu.VMEM)] * (3 + len(weights)),
        out_specs=(
            pl.BlockSpec(memory_space=pltpu.VMEM),
            pl.BlockSpec(memory_space=pltpu.VMEM),
        ),
        scratch_shapes=[
            pltpu.VMEM((padded, bottleneck), BF),
            pltpu.VMEM((padded, bottleneck), BF),
            pltpu.VMEM((count, width), BF),
            pltpu.VMEM((count, width), F32),
        ]
        + one_block
        + one_block,
        compiler_params=pltpu.CompilerParams(vmem_limit_bytes=60 * 1024 * 1024),
        cost_estimate=pl.CostEstimate(
            flops=count * 36 * width * bottleneck, bytes_accessed=24 << 20, transcendentals=0
        ),
    )(rows, targets, before, *weights)


def on_device_chains(chunks, block, activations, targets, *weights):
    axes = ("coarse", "fine")
    devices = lax.axis_size(axes)
    rows, width = activations.shape
    decoder = weights[-1]
    classes = decoder.shape[0]
    padded = jnp.pad(decoder, ((0, LANES - classes), (0, 0)))
    weights = weights[:-1] + (padded,)
    part = rows // chunks
    each = part // devices
    near = FINE_HOP * each
    far = COARSE_HOP * lax.axis_size("fine") * each

    def spread(values):
        shaped = values.reshape((devices, each) + values.shape[1:])
        moved = lax.all_to_all(shaped, axes, 0, 0, tiled=True)
        return moved.reshape(values.shape)

    spare = jnp.zeros((part, LANES - chunks), BF)
    target_tile = jnp.concatenate([targets.reshape(chunks, part).T.astype(BF), spare], axis=1)
    there = []
    for chunk in range(chunks):
        piece = activations[chunk * part : (chunk + 1) * part]
        if chunk == 0:
            piece = jnp.concatenate([piece, target_tile], axis=1)
        there.append(spread(piece))
    target_tile = there[0][:, width:]
    losses = jnp.zeros((part, LANES), BF)
    result = None
    for chunk in range(chunks):
        piece = there[chunk][:, :width]
        grad, losses = run_chains(
            piece, target_tile, losses, weights, near, far, classes, block, chunk
        )
        if chunk == chunks - 1:
            grad = jnp.concatenate([grad, losses], axis=1)
        home = spread(grad)
        if chunk == chunks - 1:
            losses = home[:, width:].astype(F32)
        place = ((chunk * part, rows - (chunk + 1) * part, 0), (0, 0, 0))
        if result is None:
            result = lax.pad(home[:, :width], jnp.zeros((), BF), place)
        else:
            result = lax.dynamic_update_slice(result, home[:, :width], (chunk * part, 0))
    summed = losses[:, : chunks * PIECES].reshape(part, chunks, PIECES).sum(axis=2)
    return (result, summed.T.reshape(rows))


def chains_fit(mesh, rows, chunks, block):
    devices = mesh.shape["coarse"] * mesh.shape["fine"]
    part = rows // chunks
    if rows % chunks or part % devices or part % block or block % LANES:
        return False
    each = part // devices
    far = COARSE_HOP * mesh.shape["fine"] * each
    return (FINE_HOP * each) % 16 == 0 and block % (FINE_HOP * each) == 0 and chunks * PIECES <= LANES and (far % block == 0 or part == block)


def solution(mesh):
    in_specs = (
        P(("coarse", "fine"), None),
        P(("coarse", "fine")),
        P(),
        P(),
        P(),
        P(),
        P(),
        P(),
        P(),
    )
    out_specs = (P(("coarse", "fine"), None), P(("coarse", "fine")))

    def step(activations, *others):
        rows = activations.shape[0] // mesh.size
        chained = chains_fit(mesh, rows, CHUNKS, BLOCK)
        body = functools.partial(on_device_chains, CHUNKS, BLOCK) if chained else on_device

        spread = jax.shard_map(
            body, mesh=mesh, in_specs=in_specs, out_specs=out_specs, check_vma=False
        )
        return spread(activations, *others)

    return step
```

```python
import functools
import math

import jax
import jax.numpy as jnp
from jax import lax
from jax.experimental import pallas as pl
from jax.experimental.pallas import tpu as pltpu
from jax.sharding import PartitionSpec as P


COARSE_HOP = 4
FINE_HOP = 2
LANES = 128
PIECES = 3
CHUNKS = 2
BLOCK = 256
WHOLE_VMEM = 60 * 1024 * 1024
SMALL_VMEM = 8 << 20


eps = 1e-05


def from_behind(value, axis, steps):
    count = lax.axis_size(axis)
    pairs = [(source, (source + steps) % count) for source in range(count)]
    return lax.ppermute(value, axis, pairs)


def norm_rows(values):
    average = jnp.mean(values, axis=-1, keepdims=True)
    centred = values - average
    factor = lax.rsqrt(jnp.mean(centred * centred, axis=-1, keepdims=True) + eps)
    return (centred * factor, factor)


def norm_back(normal, factor, upward):
    first_term = upward - jnp.mean(upward, axis=-1, keepdims=True)
    return (first_term - normal * jnp.mean(upward * normal, axis=-1, keepdims=True)) * factor


def gelu_exact(inputs):
    return 0.5 * inputs * (1.0 + lax.erf(inputs * (1.0 / math.sqrt(2.0))))


def gelu_slope(inputs):
    return 0.5 * (1.0 + lax.erf(inputs * (1.0 / math.sqrt(2.0)))) + inputs * jnp.exp(
        -0.5 * inputs * inputs
    ) * (1.0 / math.sqrt(2.0 * math.pi))


def product(leading, trailing):
    return jnp.dot(leading, trailing, preferred_element_type=jnp.float32)


def product_t(leading, trailing):
    return lax.dot_general(
        leading, trailing, (((1,), (1,)), ((), ())), preferred_element_type=jnp.float32
    )


def inner_pair(shard_rows):
    near_behind = from_behind(shard_rows, "fine", 2)
    near_ahead = from_behind(shard_rows, "fine", -2)
    far_behind = from_behind(near_behind, "coarse", 1)
    far_ahead = from_behind(near_ahead, "coarse", -1)
    fine_index = lax.axis_index("fine")
    fine_count = lax.axis_size("fine")
    behind_rows = jnp.where(fine_index < 2, far_behind, near_behind)
    ahead_rows = jnp.where(fine_index >= fine_count - 2, far_ahead, near_ahead)
    return (behind_rows, ahead_rows)


def outer_pair(shard_rows):
    behind_rows = from_behind(shard_rows, "coarse", COARSE_HOP)
    ahead_rows = from_behind(shard_rows, "coarse", -COARSE_HOP)
    return (behind_rows, ahead_rows)


def residual_block_forward(block_in, squeeze, taps, expand, neighbours):
    normal_in, _ = norm_rows(block_in.astype(jnp.float32))
    entry_act = gelu_exact(normal_in).astype(jnp.bfloat16)
    squeezed = product(entry_act, squeeze)
    normal_mid, _ = norm_rows(squeezed)
    middle = gelu_exact(normal_mid).astype(jnp.bfloat16)
    behind_rows, ahead_rows = neighbours(middle)
    conv_sum = (
        product(behind_rows, taps[0]) + product(middle, taps[1]) + product(ahead_rows, taps[2])
    )
    normal_conv, _ = norm_rows(conv_sum)
    closing = gelu_exact(normal_conv).astype(jnp.bfloat16)
    block_out = (block_in.astype(jnp.float32) + product(closing, expand)).astype(jnp.bfloat16)
    return (block_out, squeezed, conv_sum)


def residual_block_backward(
    block_in, squeezed, conv_sum, squeeze, taps, expand, neighbours, gradient_result
):
    dclosing = product_t(gradient_result.astype(jnp.bfloat16), expand)
    normal_conv, factor_conv = norm_rows(conv_sum)
    dconv = norm_back(normal_conv, factor_conv, gelu_slope(normal_conv) * dclosing).astype(
        jnp.bfloat16
    )
    behind_rows, ahead_rows = neighbours(dconv)
    dmiddle = (
        product_t(ahead_rows, taps[0]) + product_t(dconv, taps[1]) + product_t(behind_rows, taps[2])
    )
    normal_mid, factor_mid = norm_rows(squeezed)
    dsqueezed = norm_back(normal_mid, factor_mid, gelu_slope(normal_mid) * dmiddle).astype(
        jnp.bfloat16
    )
    dentry = product_t(dsqueezed, squeeze)
    normal_in, factor_in = norm_rows(block_in.astype(jnp.float32))
    return gradient_result + norm_back(normal_in, factor_in, gelu_slope(normal_in) * dentry)


def on_device(
    activations,
    targets,
    inner_squeeze_weight,
    inner_filter_taps,
    inner_expand_weight,
    outer_squeeze_weight,
    outer_filter_taps,
    outer_expand_weight,
    decoder,
):
    outer_block_input, inner_bottleneck_rows, inner_convolved = residual_block_forward(
        activations, inner_squeeze_weight, inner_filter_taps, inner_expand_weight, inner_pair
    )
    final_output, outer_bottleneck_rows, outer_convolved = residual_block_forward(
        outer_block_input, outer_squeeze_weight, outer_filter_taps, outer_expand_weight, outer_pair
    )
    normal_final, factor_final = norm_rows(final_output.astype(jnp.float32))
    normed = normal_final.astype(jnp.bfloat16)
    logits = product_t(normed, decoder)
    exponent = jnp.exp(logits)
    totals = jnp.sum(exponent, axis=-1, keepdims=True)
    classes = jnp.arange(decoder.shape[0], dtype=jnp.int32)
    onehot = (targets[:, None] == classes[None, :]).astype(jnp.float32)
    token_loss = jnp.log(totals[:, 0]) - jnp.sum(logits * onehot, axis=-1)
    dlogits = (32.0 * (exponent / totals - onehot)).astype(jnp.bfloat16)
    gradient_result = norm_back(normal_final, factor_final, product(dlogits, decoder))
    gradient_result = residual_block_backward(
        outer_block_input,
        outer_bottleneck_rows,
        outer_convolved,
        outer_squeeze_weight,
        outer_filter_taps,
        outer_expand_weight,
        outer_pair,
        gradient_result,
    )
    gradient_result = residual_block_backward(
        activations,
        inner_bottleneck_rows,
        inner_convolved,
        inner_squeeze_weight,
        inner_filter_taps,
        inner_expand_weight,
        inner_pair,
        gradient_result,
    )
    return (gradient_result.astype(jnp.bfloat16), token_loss)


BF = jnp.bfloat16
F32 = jnp.float32
ROOT_HALF = math.sqrt(0.5)
BELL = math.sqrt(2.0 / math.pi)


def scaled_norm(values, scale):
    average = jnp.mean(values, axis=-1, keepdims=True)
    centred = values - average
    factor = lax.rsqrt(jnp.mean(centred * centred, axis=-1, keepdims=True) + eps)
    return (centred * (factor * scale), factor)


def activate(values, kept, rows):
    scaled_ref, slope_ref, factor_ref = kept
    scaled, factor = scaled_norm(values, ROOT_HALF)
    half = ROOT_HALF * lax.erf(scaled) + ROOT_HALF
    scaled_ref[rows, :] = scaled
    slope_ref[rows, :] = half + scaled * (BELL * jnp.exp(-(scaled * scaled)))
    factor_ref[rows, :] = jnp.broadcast_to(factor, (factor.shape[0], LANES))
    return (scaled * half).astype(BF)


def back(upward, kept, rows):
    scaled_ref, slope_ref, factor_ref = kept
    scaled = scaled_ref[rows, :]
    through = slope_ref[rows, :] * upward
    mean = jnp.mean(through, axis=-1, keepdims=True)
    along = 2.0 * jnp.mean(through * scaled, axis=-1, keepdims=True)
    return (through - mean - scaled * along) * (factor_ref[rows, :][:, :1] * ROOT_HALF)


def chain_kernel(near, far, block, chunk, last, *refs):
    refs = list(refs)
    first_far = refs.pop(0)
    x_far = refs.pop(0) if chunk else first_far
    before_ref = refs.pop(0) if chunk else None
    *weights_far, dec_ref = refs[:7]
    refs = refs[7:]
    grad_ref = refs.pop(0)
    loss_ref = None if last else refs.pop(0)
    x_ref, ws_in, wt_in, we_in, ws_out, wt_out, we_out, target_ref = refs[:8]
    dec_pad, mid_a, mid_b, outer_in, carried = refs[8:13]
    kept = [refs[start : start + 3] for start in range(13, 31, 3)]
    in_a, mid_kept_a, con_a, in_b, mid_kept_b, con_b = kept
    sems = refs[31]
    total, width = x_ref.shape
    wide, classes = pl.ds(0, width), dec_ref.shape[0]
    starts = range(0, total, block)
    sources = [x_far.at[:, wide]] + weights_far + [first_far.at[:, pl.ds(width, LANES)]]
    copies = [
        pltpu.make_async_copy(source, target, sems.at[index])
        for index, (source, target) in enumerate(zip(sources, refs[:8]))
    ]
    for copy in copies:
        copy.start()

    dec_pad[...] = jnp.zeros_like(dec_pad)
    dec_pad[pl.ds(0, classes), :] = dec_ref[...]

    def wrap(ref):
        ref[pl.ds(0, near), :] = ref[pl.ds(total, near), :]
        ref[pl.ds(total + near, near), :] = ref[pl.ds(near, near), :]

    def near_rows(ref, start, shift):
        return ref[pl.ds(start + near + shift, block), :]

    def far_rows(ref, start, shift):
        at = (start + shift) % total
        if at + block <= total:
            return ref[pl.ds(at, block), :]
        return jnp.concatenate([ref[at:total, :], ref[: at + block - total, :]])

    def conv(behind, here, ahead, taps):
        return product(
            jnp.concatenate([behind, here, ahead], axis=1), taps[...].reshape(-1, taps.shape[2])
        )

    def conv_back(behind, here, ahead, taps):
        return product_t(
            jnp.concatenate([ahead, here, behind], axis=1),
            jnp.concatenate([taps[0], taps[1], taps[2]], axis=1),
        )

    copies[0].wait()
    copies[1].wait()
    for start in starts:
        rows = pl.ds(start, block)
        entry = activate(x_ref[rows, wide].astype(F32), in_a, rows)
        middle = activate(product(entry, ws_in[...]), mid_kept_a, rows)
        mid_a[pl.ds(start + near, block), :] = middle
    wrap(mid_a)

    for copy in copies[2:5]:
        copy.wait()
    for start in starts:
        rows = pl.ds(start, block)
        shifted = [near_rows(mid_a, start, shift) for shift in (-near, 0, near)]
        closing = activate(conv(*shifted, wt_in), con_a, rows)
        following = (x_ref[rows, wide].astype(F32) + product(closing, we_in[...])).astype(BF)
        outer_in[rows, :] = following
        entry = activate(following.astype(F32), in_b, rows)
        mid_b[rows, :] = activate(product(entry, ws_out[...]), mid_kept_b, rows)

    for copy in copies[5:]:
        copy.wait()
    for start in starts:
        rows = pl.ds(start, block)
        shifted = [far_rows(mid_b, start, shift) for shift in (-far, 0, far)]
        closing = activate(conv(*shifted, wt_out), con_b, rows)
        final = (outer_in[rows, :].astype(F32) + product(closing, we_out[...])).astype(BF)
        normal, factor = scaled_norm(final.astype(F32), 1.0)
        logits = product_t(normal.astype(BF), dec_pad[...])
        lane = lax.broadcasted_iota(jnp.int32, logits.shape, 1)
        exponent = jnp.where(lane < classes, jnp.exp(logits), 0.0)
        totals = jnp.sum(exponent, axis=-1, keepdims=True)
        target = target_ref[rows, :].astype(F32)[:, chunk : chunk + 1]
        onehot = jnp.where(lane.astype(F32) == target, 1.0, 0.0)
        loss = jnp.log(totals) - jnp.sum(logits * onehot, axis=-1, keepdims=True)
        pieces = before_ref[rows, :].astype(F32) if chunk else jnp.zeros_like(logits)
        for part in range(PIECES):
            piece = loss.astype(BF).astype(F32)
            pieces = jnp.where(lane == chunk * PIECES + part, piece, pieces)
            loss = loss - piece
        if last:
            grad_ref[rows, pl.ds(width, LANES)] = pieces.astype(BF)
        else:
            loss_ref[rows, :] = pieces.astype(BF)
        dlogits = (32.0 * (exponent / totals - onehot)).astype(BF)
        upward = norm_back(normal, factor, product(dlogits, dec_pad[...]))
        carried[rows, :] = upward
        dclosing = product_t(upward.astype(BF), we_out[...])
        mid_a[rows, :] = back(dclosing, con_b, rows).astype(BF)

    for start in starts:
        rows = pl.ds(start, block)
        shifted = [far_rows(mid_a, start, shift) for shift in (-far, 0, far)]
        dmiddle = conv_back(*shifted, wt_out)
        dsqueezed = back(dmiddle, mid_kept_b, rows).astype(BF)
        upward = carried[rows, :] + back(product_t(dsqueezed, ws_out[...]), in_b, rows)
        carried[rows, :] = upward
        dclosing = product_t(upward.astype(BF), we_in[...])
        mid_b[pl.ds(start + near, block), :] = back(dclosing, con_a, rows).astype(BF)
    wrap(mid_b)

    for start in starts:
        rows = pl.ds(start, block)
        shifted = [near_rows(mid_b, start, shift) for shift in (-near, 0, near)]
        dmiddle = conv_back(*shifted, wt_in)
        dsqueezed = back(dmiddle, mid_kept_a, rows).astype(BF)
        upward = carried[rows, :] + back(product_t(dsqueezed, ws_in[...]), in_a, rows)
        grad_ref[rows, wide] = upward.astype(BF)


VMEM = pl.BlockSpec(memory_space=pltpu.VMEM)
ANY = pl.BlockSpec(memory_space=pl.ANY)


def run_chains(first, rows, before, weights, near, far, block, chunk, last):
    count = first.shape[0]
    width, bottleneck = weights[0].shape
    padded = count + 2 * near
    tile = jax.ShapeDtypeStruct((count, LANES), BF)
    if last:
        out_shape = (jax.ShapeDtypeStruct((count, width + LANES), BF),)
    else:
        out_shape = (jax.ShapeDtypeStruct((count, width), BF), tile)

    def kept(size):
        return [
            pltpu.VMEM((count, size), F32),
            pltpu.VMEM((count, size), F32),
            pltpu.VMEM((count, LANES), F32),
        ]

    one_block = kept(width) + kept(bottleneck) + kept(bottleneck)
    operands = ((first, rows, before) if chunk else (first,)) + weights
    return pl.pallas_call(
        functools.partial(chain_kernel, near, far, block, chunk, last),
        out_shape=out_shape,
        in_specs=[ANY] * (2 if chunk else 1) + [VMEM] * (1 if chunk else 0) + [ANY] * 6 + [VMEM],
        out_specs=(VMEM,) * len(out_shape),
        scratch_shapes=[pltpu.VMEM((count, width), BF)]
        + [pltpu.VMEM(weight.shape, BF) for weight in weights[:6]]
        + [
            pltpu.VMEM((count, LANES), BF),
            pltpu.VMEM((LANES, width), BF),
            pltpu.VMEM((padded, bottleneck), BF),
            pltpu.VMEM((padded, bottleneck), BF),
            pltpu.VMEM((count, width), BF),
            pltpu.VMEM((count, width), F32),
        ]
        + one_block
        + one_block
        + [pltpu.SemaphoreType.DMA((8,))],
        compiler_params=pltpu.CompilerParams(vmem_limit_bytes=WHOLE_VMEM),
        cost_estimate=pl.CostEstimate(
            flops=count * 36 * width * bottleneck, bytes_accessed=24 << 20, transcendentals=0
        ),
    )(*operands)


def pack_kernel(x_ref, target_ref, *refs):
    outs, sems = refs[:-1], refs[-1]
    part, width = outs[-1].shape
    copies = []
    for chunk, out in enumerate(outs):
        source = x_ref.at[pl.ds(chunk * part, part), :]
        copies.append(pltpu.make_async_copy(source, out.at[:, pl.ds(0, width)], sems.at[chunk]))
        copies[-1].start()
    lane = lax.broadcasted_iota(jnp.int32, (LANES, LANES), 1)
    for start in range(0, part, LANES):
        tile = jnp.zeros((LANES, LANES), F32)
        for chunk in range(len(outs)):
            row = target_ref[pl.ds((chunk * part + start) // LANES, 1), :].astype(F32)
            column = jnp.transpose(jnp.broadcast_to(row, (LANES, LANES)))
            tile = jnp.where(lane == chunk, column, tile)
        outs[0][pl.ds(start, LANES), pl.ds(width, LANES)] = tile.astype(BF)
    for copy in copies:
        copy.wait()


def pack(activations, targets, chunks):
    rows, width = activations.shape
    part = rows // chunks
    widths = [width + LANES] + [width] * (chunks - 1)
    return pl.pallas_call(
        pack_kernel,
        out_shape=tuple(jax.ShapeDtypeStruct((part, size), BF) for size in widths),
        in_specs=[ANY, VMEM],
        out_specs=(VMEM,) * chunks,
        scratch_shapes=[pltpu.SemaphoreType.DMA((chunks,))],
        compiler_params=pltpu.CompilerParams(vmem_limit_bytes=WHOLE_VMEM),
    )(activations, targets.reshape(rows // LANES, LANES))


def unpack_kernel(*refs):
    *pieces, out_ref, loss_ref, sems = refs
    part, width = pieces[-1].shape[0], out_ref.shape[1]
    copies = []
    for chunk, piece in enumerate(pieces):
        place = out_ref.at[pl.ds(chunk * part, part), :]
        copies.append(pltpu.make_async_copy(piece.at[:, pl.ds(0, width)], place, sems.at[chunk]))
        copies[-1].start()
    for start in range(0, part, LANES):
        tile = pieces[-1][pl.ds(start, LANES), pl.ds(width, LANES)].astype(F32)
        flat = jnp.transpose(tile)
        for chunk in range(len(pieces)):
            lines = [flat[chunk * PIECES + part : chunk * PIECES + part + 1] for part in range(PIECES)]
            loss_ref[pl.ds((chunk * pieces[-1].shape[0] + start) // LANES, 1), :] = sum(
                lines[1:], lines[0]
            )
    for copy in copies:
        copy.wait()


def unpack(homes, width):
    chunks, part = len(homes), homes[0].shape[0]
    rows = chunks * part
    result, losses = pl.pallas_call(
        unpack_kernel,
        out_shape=(
            jax.ShapeDtypeStruct((rows, width), BF),
            jax.ShapeDtypeStruct((rows // LANES, LANES), F32),
        ),
        in_specs=[VMEM] * chunks,
        out_specs=(ANY, VMEM),
        scratch_shapes=[pltpu.SemaphoreType.DMA((chunks,))],
        compiler_params=pltpu.CompilerParams(vmem_limit_bytes=SMALL_VMEM),
    )(*homes)
    return (result, losses.reshape(rows))


def on_device_chains(chunks, block, activations, targets, *weights):
    axes = ("coarse", "fine")
    devices = lax.axis_size(axes)
    rows, width = activations.shape
    part = rows // chunks
    each = part // devices
    near = FINE_HOP * each
    far = COARSE_HOP * lax.axis_size("fine") * each

    def spread(values):
        shaped = values.reshape((devices, each) + values.shape[1:])
        moved = lax.all_to_all(shaped, axes, 0, 0, tiled=True)
        return moved.reshape(values.shape)

    there = []
    for piece in pack(activations, targets, chunks):
        there.append(spread(piece))
    losses = None
    homes = []
    for chunk in range(chunks):
        grad, *losses = run_chains(
            there[0], there[chunk], *(losses or [None]), weights, near, far, block, chunk,
            chunk == chunks - 1,
        )
        homes.append(spread(grad))
    return unpack(homes, width)


def chains_fit(mesh, rows, chunks, block):
    devices = mesh.shape["coarse"] * mesh.shape["fine"]
    part = rows // chunks
    if rows % chunks or part % devices or part % block or part % LANES:
        return False
    each = part // devices
    far = COARSE_HOP * mesh.shape["fine"] * each
    near = FINE_HOP * each
    return near % 16 == 0 and far % 16 == 0 and chunks * PIECES <= LANES


def solution(mesh):
    in_specs = (
        P(("coarse", "fine"), None),
        P(("coarse", "fine")),
        P(),
        P(),
        P(),
        P(),
        P(),
        P(),
        P(),
    )
    out_specs = (P(("coarse", "fine"), None), P(("coarse", "fine")))

    def step(activations, *others):
        rows = activations.shape[0] // mesh.size
        chained = chains_fit(mesh, rows, CHUNKS, BLOCK)
        body = functools.partial(on_device_chains, CHUNKS, BLOCK) if chained else on_device

        spread = jax.shard_map(
            body, mesh=mesh, in_specs=in_specs, out_specs=out_specs, check_vma=False
        )
        return spread(activations, *others)

    return step
```

```python
import functools
import math

import jax
import jax.numpy as jnp
from jax import lax
from jax.experimental import pallas as pl
from jax.experimental.pallas import tpu as pltpu
from jax.sharding import PartitionSpec as P


COARSE_HOP = 4
FINE_HOP = 2
LANES = 128
PIECES = 3
CHUNKS = 2
BLOCK = 256
WHOLE_VMEM = 60 * 1024 * 1024
SMALL_VMEM = 8 << 20


eps = 1e-05


def from_behind(value, axis, steps):
    count = lax.axis_size(axis)
    pairs = [(source, (source + steps) % count) for source in range(count)]
    return lax.ppermute(value, axis, pairs)


def norm_rows(values):
    average = jnp.mean(values, axis=-1, keepdims=True)
    centred = values - average
    factor = lax.rsqrt(jnp.mean(centred * centred, axis=-1, keepdims=True) + eps)
    return (centred * factor, factor)


def norm_back(normal, factor, upward):
    first_term = upward - jnp.mean(upward, axis=-1, keepdims=True)
    return (first_term - normal * jnp.mean(upward * normal, axis=-1, keepdims=True)) * factor


def gelu_exact(inputs):
    return 0.5 * inputs * (1.0 + lax.erf(inputs * (1.0 / math.sqrt(2.0))))


def gelu_slope(inputs):
    return 0.5 * (1.0 + lax.erf(inputs * (1.0 / math.sqrt(2.0)))) + inputs * jnp.exp(
        -0.5 * inputs * inputs
    ) * (1.0 / math.sqrt(2.0 * math.pi))


def product(leading, trailing):
    return jnp.dot(leading, trailing, preferred_element_type=jnp.float32)


def product_t(leading, trailing):
    return lax.dot_general(
        leading, trailing, (((1,), (1,)), ((), ())), preferred_element_type=jnp.float32
    )


def inner_pair(shard_rows):
    near_behind = from_behind(shard_rows, "fine", 2)
    near_ahead = from_behind(shard_rows, "fine", -2)
    far_behind = from_behind(near_behind, "coarse", 1)
    far_ahead = from_behind(near_ahead, "coarse", -1)
    fine_index = lax.axis_index("fine")
    fine_count = lax.axis_size("fine")
    behind_rows = jnp.where(fine_index < 2, far_behind, near_behind)
    ahead_rows = jnp.where(fine_index >= fine_count - 2, far_ahead, near_ahead)
    return (behind_rows, ahead_rows)


def outer_pair(shard_rows):
    behind_rows = from_behind(shard_rows, "coarse", COARSE_HOP)
    ahead_rows = from_behind(shard_rows, "coarse", -COARSE_HOP)
    return (behind_rows, ahead_rows)


def residual_block_forward(block_in, squeeze, taps, expand, neighbours):
    normal_in, _ = norm_rows(block_in.astype(jnp.float32))
    entry_act = gelu_exact(normal_in).astype(jnp.bfloat16)
    squeezed = product(entry_act, squeeze)
    normal_mid, _ = norm_rows(squeezed)
    middle = gelu_exact(normal_mid).astype(jnp.bfloat16)
    behind_rows, ahead_rows = neighbours(middle)
    conv_sum = (
        product(behind_rows, taps[0]) + product(middle, taps[1]) + product(ahead_rows, taps[2])
    )
    normal_conv, _ = norm_rows(conv_sum)
    closing = gelu_exact(normal_conv).astype(jnp.bfloat16)
    block_out = (block_in.astype(jnp.float32) + product(closing, expand)).astype(jnp.bfloat16)
    return (block_out, squeezed, conv_sum)


def residual_block_backward(
    block_in, squeezed, conv_sum, squeeze, taps, expand, neighbours, gradient_result
):
    dclosing = product_t(gradient_result.astype(jnp.bfloat16), expand)
    normal_conv, factor_conv = norm_rows(conv_sum)
    dconv = norm_back(normal_conv, factor_conv, gelu_slope(normal_conv) * dclosing).astype(
        jnp.bfloat16
    )
    behind_rows, ahead_rows = neighbours(dconv)
    dmiddle = (
        product_t(ahead_rows, taps[0]) + product_t(dconv, taps[1]) + product_t(behind_rows, taps[2])
    )
    normal_mid, factor_mid = norm_rows(squeezed)
    dsqueezed = norm_back(normal_mid, factor_mid, gelu_slope(normal_mid) * dmiddle).astype(
        jnp.bfloat16
    )
    dentry = product_t(dsqueezed, squeeze)
    normal_in, factor_in = norm_rows(block_in.astype(jnp.float32))
    return gradient_result + norm_back(normal_in, factor_in, gelu_slope(normal_in) * dentry)


def on_device(
    activations,
    targets,
    inner_squeeze_weight,
    inner_filter_taps,
    inner_expand_weight,
    outer_squeeze_weight,
    outer_filter_taps,
    outer_expand_weight,
    decoder,
):
    outer_block_input, inner_bottleneck_rows, inner_convolved = residual_block_forward(
        activations, inner_squeeze_weight, inner_filter_taps, inner_expand_weight, inner_pair
    )
    final_output, outer_bottleneck_rows, outer_convolved = residual_block_forward(
        outer_block_input, outer_squeeze_weight, outer_filter_taps, outer_expand_weight, outer_pair
    )
    normal_final, factor_final = norm_rows(final_output.astype(jnp.float32))
    normed = normal_final.astype(jnp.bfloat16)
    logits = product_t(normed, decoder)
    exponent = jnp.exp(logits)
    totals = jnp.sum(exponent, axis=-1, keepdims=True)
    classes = jnp.arange(decoder.shape[0], dtype=jnp.int32)
    onehot = (targets[:, None] == classes[None, :]).astype(jnp.float32)
    token_loss = jnp.log(totals[:, 0]) - jnp.sum(logits * onehot, axis=-1)
    dlogits = (32.0 * (exponent / totals - onehot)).astype(jnp.bfloat16)
    gradient_result = norm_back(normal_final, factor_final, product(dlogits, decoder))
    gradient_result = residual_block_backward(
        outer_block_input,
        outer_bottleneck_rows,
        outer_convolved,
        outer_squeeze_weight,
        outer_filter_taps,
        outer_expand_weight,
        outer_pair,
        gradient_result,
    )
    gradient_result = residual_block_backward(
        activations,
        inner_bottleneck_rows,
        inner_convolved,
        inner_squeeze_weight,
        inner_filter_taps,
        inner_expand_weight,
        inner_pair,
        gradient_result,
    )
    return (gradient_result.astype(jnp.bfloat16), token_loss)


BF = jnp.bfloat16
F32 = jnp.float32
ROOT_HALF = math.sqrt(0.5)
BELL = math.sqrt(2.0 / math.pi)


def scaled_norm(values, scale):
    average = jnp.mean(values, axis=-1, keepdims=True)
    centred = values - average
    factor = lax.rsqrt(jnp.mean(centred * centred, axis=-1, keepdims=True) + eps)
    return (centred * (factor * scale), factor)


def activate(values, kept, rows):
    scaled_ref, slope_ref, factor_ref = kept
    scaled, factor = scaled_norm(values, ROOT_HALF)
    half = ROOT_HALF * lax.erf(scaled) + ROOT_HALF
    scaled_ref[rows, :] = scaled
    slope_ref[rows, :] = half + scaled * (BELL * jnp.exp(-(scaled * scaled)))
    factor_ref[rows, :] = jnp.broadcast_to(factor, (factor.shape[0], LANES))
    return (scaled * half).astype(BF)


def back(upward, kept, rows):
    scaled_ref, slope_ref, factor_ref = kept
    scaled = scaled_ref[rows, :]
    through = slope_ref[rows, :] * upward
    mean = jnp.mean(through, axis=-1, keepdims=True)
    along = 2.0 * jnp.mean(through * scaled, axis=-1, keepdims=True)
    return (through - mean - scaled * along) * (factor_ref[rows, :][:, :1] * ROOT_HALF)


def chain_kernel(near, far, block, chunk, last, *refs):
    refs = list(refs)
    x_far = refs.pop(0)
    target_ref = refs.pop(0)
    before_ref = refs.pop(0) if chunk else None
    *weights_far, dec_ref = refs[:7]
    refs = refs[7:]
    grad_ref = refs.pop(0)
    loss_ref = None if last else refs.pop(0)
    x_ref, ws_in, wt_in, we_in, ws_out, wt_out, we_out = refs[:7]
    dec_pad, mid_a, mid_b, outer_in, carried = refs[7:12]
    kept = [refs[start : start + 3] for start in range(12, 30, 3)]
    in_a, mid_kept_a, con_a, in_b, mid_kept_b, con_b = kept
    sems = refs[30]
    total, width = x_ref.shape
    wide, classes = pl.ds(0, width), dec_ref.shape[0]
    starts = range(0, total, block)
    sources = [x_far] + weights_far
    copies = [
        pltpu.make_async_copy(source, target, sems.at[index])
        for index, (source, target) in enumerate(zip(sources, refs[:7]))
    ]
    for copy in copies[:2]:
        copy.start()

    dec_pad[...] = jnp.zeros_like(dec_pad)
    dec_pad[pl.ds(0, classes), :] = dec_ref[...]

    def wrap(ref):
        ref[pl.ds(0, near), :] = ref[pl.ds(total, near), :]
        ref[pl.ds(total + near, near), :] = ref[pl.ds(near, near), :]

    def near_rows(ref, start, shift):
        return ref[pl.ds(start + near + shift, block), :]

    def far_rows(ref, start, shift):
        at = (start + shift) % total
        if at + block <= total:
            return ref[pl.ds(at, block), :]
        return jnp.concatenate([ref[at:total, :], ref[: at + block - total, :]])

    def conv(behind, here, ahead, taps):
        return product(
            jnp.concatenate([behind, here, ahead], axis=1), taps[...].reshape(-1, taps.shape[2])
        )

    def conv_back(behind, here, ahead, taps):
        return product_t(
            jnp.concatenate([ahead, here, behind], axis=1),
            jnp.concatenate([taps[0], taps[1], taps[2]], axis=1),
        )

    for copy in copies[:2]:
        copy.wait()
    for copy in copies[2:]:
        copy.start()
    for start in starts:
        rows = pl.ds(start, block)
        entry = activate(x_ref[rows, :].astype(F32), in_a, rows)
        middle = activate(product(entry, ws_in[...]), mid_kept_a, rows)
        mid_a[pl.ds(start + near, block), :] = middle
    wrap(mid_a)

    for copy in copies[2:5]:
        copy.wait()
    for start in starts:
        rows = pl.ds(start, block)
        shifted = [near_rows(mid_a, start, shift) for shift in (-near, 0, near)]
        closing = activate(conv(*shifted, wt_in), con_a, rows)
        following = (x_ref[rows, :].astype(F32) + product(closing, we_in[...])).astype(BF)
        outer_in[rows, :] = following
        entry = activate(following.astype(F32), in_b, rows)
        mid_b[rows, :] = activate(product(entry, ws_out[...]), mid_kept_b, rows)

    for copy in copies[5:]:
        copy.wait()
    for start in starts:
        rows = pl.ds(start, block)
        shifted = [far_rows(mid_b, start, shift) for shift in (-far, 0, far)]
        closing = activate(conv(*shifted, wt_out), con_b, rows)
        final = (outer_in[rows, :].astype(F32) + product(closing, we_out[...])).astype(BF)
        normal, factor = scaled_norm(final.astype(F32), 1.0)
        logits = product_t(normal.astype(BF), dec_pad[...])
        lane = lax.broadcasted_iota(jnp.int32, logits.shape, 1)
        exponent = jnp.where(lane < classes, jnp.exp(logits), 0.0)
        totals = jnp.sum(exponent, axis=-1, keepdims=True)
        target = target_ref[rows, :].astype(F32)[:, chunk : chunk + 1]
        onehot = jnp.where(lane.astype(F32) == target, 1.0, 0.0)
        loss = jnp.log(totals) - jnp.sum(logits * onehot, axis=-1, keepdims=True)
        pieces = before_ref[rows, :].astype(F32) if chunk else jnp.zeros_like(logits)
        for part in range(PIECES):
            piece = loss.astype(BF).astype(F32)
            pieces = jnp.where(lane == chunk * PIECES + part, piece, pieces)
            loss = loss - piece
        if last:
            grad_ref[rows, pl.ds(width, LANES)] = pieces.astype(BF)
        else:
            loss_ref[rows, :] = pieces.astype(BF)
        dlogits = (32.0 * (exponent / totals - onehot)).astype(BF)
        upward = norm_back(normal, factor, product(dlogits, dec_pad[...]))
        carried[rows, :] = upward
        dclosing = product_t(upward.astype(BF), we_out[...])
        mid_a[rows, :] = back(dclosing, con_b, rows).astype(BF)

    for start in starts:
        rows = pl.ds(start, block)
        shifted = [far_rows(mid_a, start, shift) for shift in (-far, 0, far)]
        dmiddle = conv_back(*shifted, wt_out)
        dsqueezed = back(dmiddle, mid_kept_b, rows).astype(BF)
        upward = carried[rows, :] + back(product_t(dsqueezed, ws_out[...]), in_b, rows)
        carried[rows, :] = upward
        dclosing = product_t(upward.astype(BF), we_in[...])
        mid_b[pl.ds(start + near, block), :] = back(dclosing, con_a, rows).astype(BF)
    wrap(mid_b)

    for start in starts:
        rows = pl.ds(start, block)
        shifted = [near_rows(mid_b, start, shift) for shift in (-near, 0, near)]
        dmiddle = conv_back(*shifted, wt_in)
        dsqueezed = back(dmiddle, mid_kept_a, rows).astype(BF)
        upward = carried[rows, :] + back(product_t(dsqueezed, ws_in[...]), in_a, rows)
        grad_ref[rows, wide] = upward.astype(BF)


VMEM = pl.BlockSpec(memory_space=pltpu.VMEM)
ANY = pl.BlockSpec(memory_space=pl.ANY)


def run_chains(rows, carried, weights, near, far, block, chunk, last):
    count = rows.shape[0]
    width, bottleneck = weights[0].shape
    padded = count + 2 * near
    tile = jax.ShapeDtypeStruct((count, LANES), BF)
    if last:
        out_shape = (jax.ShapeDtypeStruct((count, width + LANES), BF),)
    else:
        out_shape = (jax.ShapeDtypeStruct((count, width), BF), tile)

    def kept(size):
        return [
            pltpu.VMEM((count, size), F32),
            pltpu.VMEM((count, size), F32),
            pltpu.VMEM((count, LANES), F32),
        ]

    one_block = kept(width) + kept(bottleneck) + kept(bottleneck)
    operands = (rows,) + carried + weights
    return pl.pallas_call(
        functools.partial(chain_kernel, near, far, block, chunk, last),
        out_shape=out_shape,
        in_specs=[ANY] + [VMEM] * len(carried) + [ANY] * 6 + [VMEM],
        out_specs=(VMEM,) * len(out_shape),
        scratch_shapes=[pltpu.VMEM((count, width), BF)]
        + [pltpu.VMEM(weight.shape, BF) for weight in weights[:6]]
        + [
            pltpu.VMEM((LANES, width), BF),
            pltpu.VMEM((padded, bottleneck), BF),
            pltpu.VMEM((padded, bottleneck), BF),
            pltpu.VMEM((count, width), BF),
            pltpu.VMEM((count, width), F32),
        ]
        + one_block
        + one_block
        + [pltpu.SemaphoreType.DMA((7,))],
        compiler_params=pltpu.CompilerParams(vmem_limit_bytes=WHOLE_VMEM),
        cost_estimate=pl.CostEstimate(
            flops=count * 36 * width * bottleneck, bytes_accessed=24 << 20, transcendentals=0
        ),
    )(*operands)


def unpack_kernel(*refs):
    *pieces, out_ref, loss_ref, sems = refs
    part, width = pieces[-1].shape[0], out_ref.shape[1]
    copies = []
    for chunk, piece in enumerate(pieces):
        place = out_ref.at[pl.ds(chunk * part, part), :]
        copies.append(pltpu.make_async_copy(piece.at[:, pl.ds(0, width)], place, sems.at[chunk]))
        copies[-1].start()
    for start in range(0, part, LANES):
        tile = pieces[-1][pl.ds(start, LANES), pl.ds(width, LANES)].astype(F32)
        flat = jnp.transpose(tile)
        for chunk in range(len(pieces)):
            lines = [flat[chunk * PIECES + part : chunk * PIECES + part + 1] for part in range(PIECES)]
            loss_ref[pl.ds((chunk * pieces[-1].shape[0] + start) // LANES, 1), :] = sum(
                lines[1:], lines[0]
            )
    for copy in copies:
        copy.wait()


def unpack(homes, width):
    chunks, part = len(homes), homes[0].shape[0]
    rows = chunks * part
    result, losses = pl.pallas_call(
        unpack_kernel,
        out_shape=(
            jax.ShapeDtypeStruct((rows, width), BF),
            jax.ShapeDtypeStruct((rows // LANES, LANES), F32),
        ),
        in_specs=[VMEM] * chunks,
        out_specs=(ANY, VMEM),
        scratch_shapes=[pltpu.SemaphoreType.DMA((chunks,))],
        compiler_params=pltpu.CompilerParams(vmem_limit_bytes=SMALL_VMEM),
    )(*homes)
    return (result, losses.reshape(rows))


def on_device_chains(chunks, block, activations, targets, *weights):
    axes = ("coarse", "fine")
    devices = lax.axis_size(axes)
    rows, width = activations.shape
    part = rows // chunks
    each = part // devices
    near = FINE_HOP * each
    far = COARSE_HOP * lax.axis_size("fine") * each

    def spread(values):
        shaped = values.reshape((devices, each) + values.shape[1:])
        moved = lax.all_to_all(shaped, axes, 0, 0, tiled=True)
        return moved.reshape(values.shape)

    def gathered(values):
        parts = values[None]
        me = lax.axis_index(axes)
        while parts.shape[0] < devices:
            distance = parts.shape[0]
            pairs = [(source, source ^ distance) for source in range(devices)]
            got = lax.ppermute(parts, axes, pairs)
            upper = lax.bitwise_and(me, distance) > 0
            parts = jnp.where(
                upper, jnp.concatenate([got, parts]), jnp.concatenate([parts, got])
            )
        return parts

    there = [spread(activations[:part])]
    everyone = lax.optimization_barrier(gathered(targets)).reshape(devices, chunks, devices, each)
    mine = lax.dynamic_slice_in_dim(everyone, lax.axis_index(axes), 1, axis=2)
    columns = mine.transpose(0, 3, 1, 2).reshape(part, chunks).astype(BF)
    tile = jnp.pad(columns, ((0, 0), (0, LANES - chunks)))
    held, tile = lax.optimization_barrier((activations, tile))
    for chunk in range(1, chunks):
        there.append(spread(held[chunk * part : (chunk + 1) * part]))
    losses = ()
    homes = []
    for chunk in range(chunks):
        grad, *losses = run_chains(
            there[chunk], (tile, *losses), weights, near, far, block, chunk, chunk == chunks - 1
        )
        homes.append(spread(grad))
    return unpack(homes, width)


def chains_fit(mesh, rows, chunks, block):
    devices = mesh.shape["coarse"] * mesh.shape["fine"]
    part = rows // chunks
    if rows % chunks or part % devices or part % block or part % LANES:
        return False
    each = part // devices
    far = COARSE_HOP * mesh.shape["fine"] * each
    near = FINE_HOP * each
    paired = devices & (devices - 1) == 0
    return paired and near % 16 == 0 and far % 16 == 0 and chunks * PIECES <= LANES


def solution(mesh):
    in_specs = (
        P(("coarse", "fine"), None),
        P(("coarse", "fine")),
        P(),
        P(),
        P(),
        P(),
        P(),
        P(),
        P(),
    )
    out_specs = (P(("coarse", "fine"), None), P(("coarse", "fine")))

    def step(activations, *others):
        rows = activations.shape[0] // mesh.size
        chained = chains_fit(mesh, rows, CHUNKS, BLOCK)
        body = functools.partial(on_device_chains, CHUNKS, BLOCK) if chained else on_device

        spread = jax.shard_map(
            body, mesh=mesh, in_specs=in_specs, out_specs=out_specs, check_vma=False
        )
        return spread(activations, *others)

    return step
```

```python
import functools
import math

import jax
import jax.numpy as jnp
from jax import lax
from jax.experimental import pallas as pl
from jax.experimental.pallas import tpu as pltpu
from jax.sharding import PartitionSpec as P


COARSE_HOP = 4
FINE_HOP = 2
LANES = 128
PIECES = 3
CHUNKS = 2
BLOCK = 256
WHOLE_VMEM = 60 * 1024 * 1024
KERNEL_VMEM = 52500 << 10
SMALL_VMEM = 8 << 20


eps = 1e-05


def from_behind(value, axis, steps):
    count = lax.axis_size(axis)
    pairs = [(source, (source + steps) % count) for source in range(count)]
    return lax.ppermute(value, axis, pairs)


def norm_rows(values):
    average = jnp.mean(values, axis=-1, keepdims=True)
    centred = values - average
    factor = lax.rsqrt(jnp.mean(centred * centred, axis=-1, keepdims=True) + eps)
    return (centred * factor, factor)


def norm_back(normal, factor, upward):
    first_term = upward - jnp.mean(upward, axis=-1, keepdims=True)
    return (first_term - normal * jnp.mean(upward * normal, axis=-1, keepdims=True)) * factor


def gelu_exact(inputs):
    return 0.5 * inputs * (1.0 + lax.erf(inputs * (1.0 / math.sqrt(2.0))))


def gelu_slope(inputs):
    return 0.5 * (1.0 + lax.erf(inputs * (1.0 / math.sqrt(2.0)))) + inputs * jnp.exp(
        -0.5 * inputs * inputs
    ) * (1.0 / math.sqrt(2.0 * math.pi))


def product(leading, trailing):
    return jnp.dot(leading, trailing, preferred_element_type=jnp.float32)


def product_t(leading, trailing):
    return lax.dot_general(
        leading, trailing, (((1,), (1,)), ((), ())), preferred_element_type=jnp.float32
    )


def inner_pair(shard_rows):
    near_behind = from_behind(shard_rows, "fine", 2)
    near_ahead = from_behind(shard_rows, "fine", -2)
    far_behind = from_behind(near_behind, "coarse", 1)
    far_ahead = from_behind(near_ahead, "coarse", -1)
    fine_index = lax.axis_index("fine")
    fine_count = lax.axis_size("fine")
    behind_rows = jnp.where(fine_index < 2, far_behind, near_behind)
    ahead_rows = jnp.where(fine_index >= fine_count - 2, far_ahead, near_ahead)
    return (behind_rows, ahead_rows)


def outer_pair(shard_rows):
    behind_rows = from_behind(shard_rows, "coarse", COARSE_HOP)
    ahead_rows = from_behind(shard_rows, "coarse", -COARSE_HOP)
    return (behind_rows, ahead_rows)


def residual_block_forward(block_in, squeeze, taps, expand, neighbours):
    normal_in, _ = norm_rows(block_in.astype(jnp.float32))
    entry_act = gelu_exact(normal_in).astype(jnp.bfloat16)
    squeezed = product(entry_act, squeeze)
    normal_mid, _ = norm_rows(squeezed)
    middle = gelu_exact(normal_mid).astype(jnp.bfloat16)
    behind_rows, ahead_rows = neighbours(middle)
    conv_sum = (
        product(behind_rows, taps[0]) + product(middle, taps[1]) + product(ahead_rows, taps[2])
    )
    normal_conv, _ = norm_rows(conv_sum)
    closing = gelu_exact(normal_conv).astype(jnp.bfloat16)
    block_out = (block_in.astype(jnp.float32) + product(closing, expand)).astype(jnp.bfloat16)
    return (block_out, squeezed, conv_sum)


def residual_block_backward(
    block_in, squeezed, conv_sum, squeeze, taps, expand, neighbours, gradient_result
):
    dclosing = product_t(gradient_result.astype(jnp.bfloat16), expand)
    normal_conv, factor_conv = norm_rows(conv_sum)
    dconv = norm_back(normal_conv, factor_conv, gelu_slope(normal_conv) * dclosing).astype(
        jnp.bfloat16
    )
    behind_rows, ahead_rows = neighbours(dconv)
    dmiddle = (
        product_t(ahead_rows, taps[0]) + product_t(dconv, taps[1]) + product_t(behind_rows, taps[2])
    )
    normal_mid, factor_mid = norm_rows(squeezed)
    dsqueezed = norm_back(normal_mid, factor_mid, gelu_slope(normal_mid) * dmiddle).astype(
        jnp.bfloat16
    )
    dentry = product_t(dsqueezed, squeeze)
    normal_in, factor_in = norm_rows(block_in.astype(jnp.float32))
    return gradient_result + norm_back(normal_in, factor_in, gelu_slope(normal_in) * dentry)


def on_device(
    activations,
    targets,
    inner_squeeze_weight,
    inner_filter_taps,
    inner_expand_weight,
    outer_squeeze_weight,
    outer_filter_taps,
    outer_expand_weight,
    decoder,
):
    outer_block_input, inner_bottleneck_rows, inner_convolved = residual_block_forward(
        activations, inner_squeeze_weight, inner_filter_taps, inner_expand_weight, inner_pair
    )
    final_output, outer_bottleneck_rows, outer_convolved = residual_block_forward(
        outer_block_input, outer_squeeze_weight, outer_filter_taps, outer_expand_weight, outer_pair
    )
    normal_final, factor_final = norm_rows(final_output.astype(jnp.float32))
    normed = normal_final.astype(jnp.bfloat16)
    logits = product_t(normed, decoder)
    exponent = jnp.exp(logits)
    totals = jnp.sum(exponent, axis=-1, keepdims=True)
    classes = jnp.arange(decoder.shape[0], dtype=jnp.int32)
    onehot = (targets[:, None] == classes[None, :]).astype(jnp.float32)
    token_loss = jnp.log(totals[:, 0]) - jnp.sum(logits * onehot, axis=-1)
    dlogits = (32.0 * (exponent / totals - onehot)).astype(jnp.bfloat16)
    gradient_result = norm_back(normal_final, factor_final, product(dlogits, decoder))
    gradient_result = residual_block_backward(
        outer_block_input,
        outer_bottleneck_rows,
        outer_convolved,
        outer_squeeze_weight,
        outer_filter_taps,
        outer_expand_weight,
        outer_pair,
        gradient_result,
    )
    gradient_result = residual_block_backward(
        activations,
        inner_bottleneck_rows,
        inner_convolved,
        inner_squeeze_weight,
        inner_filter_taps,
        inner_expand_weight,
        inner_pair,
        gradient_result,
    )
    return (gradient_result.astype(jnp.bfloat16), token_loss)


BF = jnp.bfloat16
F32 = jnp.float32
ROOT_HALF = math.sqrt(0.5)
BELL = math.sqrt(2.0 / math.pi)


def scaled_norm(values, scale):
    average = jnp.mean(values, axis=-1, keepdims=True)
    centred = values - average
    factor = lax.rsqrt(jnp.mean(centred * centred, axis=-1, keepdims=True) + eps)
    return (centred * (factor * scale), factor)


def activate(values, kept, rows):
    scaled_ref, slope_ref, factor_ref = kept
    scaled, factor = scaled_norm(values, ROOT_HALF)
    half = ROOT_HALF * lax.erf(scaled) + ROOT_HALF
    scaled_ref[rows, :] = scaled
    slope_ref[rows, :] = half + scaled * (BELL * jnp.exp(-(scaled * scaled)))
    factor_ref[rows, :] = jnp.broadcast_to(factor, (factor.shape[0], LANES))
    return (scaled * half).astype(BF)


def back(upward, kept, rows):
    scaled_ref, slope_ref, factor_ref = kept
    scaled = scaled_ref[rows, :]
    through = slope_ref[rows, :] * upward
    mean = jnp.mean(through, axis=-1, keepdims=True)
    along = 2.0 * jnp.mean(through * scaled, axis=-1, keepdims=True)
    return (through - mean - scaled * along) * (factor_ref[rows, :][:, :1] * ROOT_HALF)


def chain_kernel(near, far, block, chunk, last, *refs):
    refs = list(refs)
    first_ref = refs.pop(0)
    x_ref = refs.pop(0) if chunk else first_ref
    before_ref = refs.pop(0) if chunk else None
    *weights_far, dec_ref = refs[:7]
    refs = refs[7:]
    grad_ref = refs.pop(0)
    loss_ref = None if last else refs.pop(0)
    ws_in, wt_in, we_in, ws_out, wt_out, we_out = refs[:6]
    dec_pad, mid_a, mid_b, outer_in, carried = refs[6:11]
    kept = [refs[start : start + 3] for start in range(11, 29, 3)]
    in_a, mid_kept_a, con_a, in_b, mid_kept_b, con_b = kept
    sems = refs[29]
    total, width = x_ref.shape[0], ws_in.shape[0]
    wide, classes = pl.ds(0, width), dec_ref.shape[0]
    starts = range(0, total, block)
    copies = [
        pltpu.make_async_copy(source, target, sems.at[index])
        for index, (source, target) in enumerate(zip(weights_far, refs[:6]))
    ]
    for copy in copies:
        copy.start()

    dec_pad[...] = jnp.zeros_like(dec_pad)
    dec_pad[pl.ds(0, classes), :] = dec_ref[...]

    def wrap(ref):
        ref[pl.ds(0, near), :] = ref[pl.ds(total, near), :]
        ref[pl.ds(total + near, near), :] = ref[pl.ds(near, near), :]

    def near_rows(ref, start, shift):
        return ref[pl.ds(start + near + shift, block), :]

    def far_rows(ref, start, shift):
        at = (start + shift) % total
        if at + block <= total:
            return ref[pl.ds(at, block), :]
        return jnp.concatenate([ref[at:total, :], ref[: at + block - total, :]])

    def conv(behind, here, ahead, taps):
        return product(
            jnp.concatenate([behind, here, ahead], axis=1), taps[...].reshape(-1, taps.shape[2])
        )

    def conv_back(behind, here, ahead, taps):
        return product_t(
            jnp.concatenate([ahead, here, behind], axis=1),
            jnp.concatenate([taps[0], taps[1], taps[2]], axis=1),
        )

    for start in starts:
        rows = pl.ds(start, block)
        entry = activate(x_ref[rows, wide].astype(F32), in_a, rows)
        if start == 0:
            copies[0].wait()
        middle = activate(product(entry, ws_in[...]), mid_kept_a, rows)
        mid_a[pl.ds(start + near, block), :] = middle
    wrap(mid_a)

    for copy in copies[1:4]:
        copy.wait()
    for start in starts:
        rows = pl.ds(start, block)
        shifted = [near_rows(mid_a, start, shift) for shift in (-near, 0, near)]
        closing = activate(conv(*shifted, wt_in), con_a, rows)
        following = (x_ref[rows, wide].astype(F32) + product(closing, we_in[...])).astype(BF)
        outer_in[rows, :] = following
        entry = activate(following.astype(F32), in_b, rows)
        mid_b[rows, :] = activate(product(entry, ws_out[...]), mid_kept_b, rows)

    for copy in copies[4:]:
        copy.wait()
    for start in starts:
        rows = pl.ds(start, block)
        shifted = [far_rows(mid_b, start, shift) for shift in (-far, 0, far)]
        closing = activate(conv(*shifted, wt_out), con_b, rows)
        final = (outer_in[rows, :].astype(F32) + product(closing, we_out[...])).astype(BF)
        normal, factor = scaled_norm(final.astype(F32), 1.0)
        logits = product_t(normal.astype(BF), dec_pad[...])
        lane = lax.broadcasted_iota(jnp.int32, logits.shape, 1)
        exponent = jnp.where(lane < classes, jnp.exp(logits), 0.0)
        totals = jnp.sum(exponent, axis=-1, keepdims=True)
        target = first_ref[rows, pl.ds(width, LANES)].astype(F32)[:, chunk : chunk + 1]
        onehot = jnp.where(lane.astype(F32) == target, 1.0, 0.0)
        loss = jnp.log(totals) - jnp.sum(logits * onehot, axis=-1, keepdims=True)
        pieces = before_ref[rows, :].astype(F32) if chunk else jnp.zeros_like(logits)
        for part in range(PIECES):
            piece = loss.astype(BF).astype(F32)
            pieces = jnp.where(lane == chunk * PIECES + part, piece, pieces)
            loss = loss - piece
        if last:
            grad_ref[rows, pl.ds(width, LANES)] = pieces.astype(BF)
        else:
            loss_ref[rows, :] = pieces.astype(BF)
        dlogits = (32.0 * (exponent / totals - onehot)).astype(BF)
        upward = norm_back(normal, factor, product(dlogits, dec_pad[...]))
        carried[rows, :] = upward
        dclosing = product_t(upward.astype(BF), we_out[...])
        mid_a[rows, :] = back(dclosing, con_b, rows).astype(BF)

    for start in starts:
        rows = pl.ds(start, block)
        shifted = [far_rows(mid_a, start, shift) for shift in (-far, 0, far)]
        dmiddle = conv_back(*shifted, wt_out)
        dsqueezed = back(dmiddle, mid_kept_b, rows).astype(BF)
        upward = carried[rows, :] + back(product_t(dsqueezed, ws_out[...]), in_b, rows)
        carried[rows, :] = upward
        dclosing = product_t(upward.astype(BF), we_in[...])
        mid_b[pl.ds(start + near, block), :] = back(dclosing, con_a, rows).astype(BF)
    wrap(mid_b)

    for start in starts:
        rows = pl.ds(start, block)
        shifted = [near_rows(mid_b, start, shift) for shift in (-near, 0, near)]
        dmiddle = conv_back(*shifted, wt_in)
        dsqueezed = back(dmiddle, mid_kept_a, rows).astype(BF)
        upward = carried[rows, :] + back(product_t(dsqueezed, ws_in[...]), in_a, rows)
        grad_ref[rows, wide] = upward.astype(BF)


VMEM = pl.BlockSpec(memory_space=pltpu.VMEM)
ANY = pl.BlockSpec(memory_space=pl.ANY)


def run_chains(first, rows, before, weights, near, far, block, chunk, last):
    count = first.shape[0]
    width, bottleneck = weights[0].shape
    padded = count + 2 * near
    tile = jax.ShapeDtypeStruct((count, LANES), BF)
    if last:
        out_shape = (jax.ShapeDtypeStruct((count, width + LANES), BF),)
    else:
        out_shape = (jax.ShapeDtypeStruct((count, width), BF), tile)

    def kept(size):
        return [
            pltpu.VMEM((count, size), F32),
            pltpu.VMEM((count, size), F32),
            pltpu.VMEM((count, LANES), F32),
        ]

    one_block = kept(width) + kept(bottleneck) + kept(bottleneck)
    operands = ((first, rows, before) if chunk else (first,)) + weights
    return pl.pallas_call(
        functools.partial(chain_kernel, near, far, block, chunk, last),
        out_shape=out_shape,
        in_specs=[VMEM] * (3 if chunk else 1) + [ANY] * 6 + [VMEM],
        out_specs=(VMEM,) * len(out_shape),
        scratch_shapes=[pltpu.VMEM(weight.shape, BF) for weight in weights[:6]]
        + [
            pltpu.VMEM((LANES, width), BF),
            pltpu.VMEM((padded, bottleneck), BF),
            pltpu.VMEM((padded, bottleneck), BF),
            pltpu.VMEM((count, width), BF),
            pltpu.VMEM((count, width), F32),
        ]
        + one_block
        + one_block
        + [pltpu.SemaphoreType.DMA((6,))],
        compiler_params=pltpu.CompilerParams(vmem_limit_bytes=KERNEL_VMEM),
        cost_estimate=pl.CostEstimate(
            flops=count * 36 * width * bottleneck, bytes_accessed=24 << 20, transcendentals=0
        ),
    )(*operands)


def pack_kernel(chunks, x_ref, target_ref, out_ref, sems):
    part, width = out_ref.shape[0], x_ref.shape[1]
    source = x_ref.at[pl.ds(0, part), :]
    copy = pltpu.make_async_copy(source, out_ref.at[:, pl.ds(0, width)], sems.at[0])
    copy.start()
    lane = lax.broadcasted_iota(jnp.int32, (LANES, LANES), 1)
    for start in range(0, part, LANES):
        tile = jnp.zeros((LANES, LANES), F32)
        for chunk in range(chunks):
            row = target_ref[pl.ds((chunk * part + start) // LANES, 1), :].astype(F32)
            column = jnp.transpose(jnp.broadcast_to(row, (LANES, LANES)))
            tile = jnp.where(lane == chunk, column, tile)
        out_ref[pl.ds(start, LANES), pl.ds(width, LANES)] = tile.astype(BF)
    copy.wait()


def pack(activations, targets, chunks):
    rows, width = activations.shape
    return pl.pallas_call(
        functools.partial(pack_kernel, chunks),
        out_shape=jax.ShapeDtypeStruct((rows // chunks, width + LANES), BF),
        in_specs=[ANY, VMEM],
        out_specs=VMEM,
        scratch_shapes=[pltpu.SemaphoreType.DMA((1,))],
        compiler_params=pltpu.CompilerParams(vmem_limit_bytes=WHOLE_VMEM),
    )(activations, targets.reshape(rows // LANES, LANES))


def rest_kernel(x_ref, *refs):
    outs, sems = refs[:-1], refs[-1]
    part = outs[0].shape[0]
    copies = [
        pltpu.make_async_copy(x_ref.at[pl.ds((chunk + 1) * part, part), :], out, sems.at[chunk])
        for chunk, out in enumerate(outs)
    ]
    for copy in copies:
        copy.start()
    for copy in copies:
        copy.wait()


def rest(activations, chunks):
    rows, width = activations.shape
    return pl.pallas_call(
        rest_kernel,
        out_shape=(jax.ShapeDtypeStruct((rows // chunks, width), BF),) * (chunks - 1),
        in_specs=[ANY],
        out_specs=(VMEM,) * (chunks - 1),
        scratch_shapes=[pltpu.SemaphoreType.DMA((chunks - 1,))],
        compiler_params=pltpu.CompilerParams(vmem_limit_bytes=WHOLE_VMEM),
    )(activations)


def unpack_kernel(*refs):
    *pieces, out_ref, loss_ref, sems = refs
    part, width = pieces[-1].shape[0], out_ref.shape[1]
    copies = []
    for chunk, piece in enumerate(pieces):
        place = out_ref.at[pl.ds(chunk * part, part), :]
        copies.append(pltpu.make_async_copy(piece.at[:, pl.ds(0, width)], place, sems.at[chunk]))
        copies[-1].start()
    for start in range(0, part, LANES):
        tile = pieces[-1][pl.ds(start, LANES), pl.ds(width, LANES)].astype(F32)
        flat = jnp.transpose(tile)
        for chunk in range(len(pieces)):
            lines = [flat[chunk * PIECES + part : chunk * PIECES + part + 1] for part in range(PIECES)]
            loss_ref[pl.ds((chunk * pieces[-1].shape[0] + start) // LANES, 1), :] = sum(
                lines[1:], lines[0]
            )
    for copy in copies:
        copy.wait()


def unpack(homes, width):
    chunks, part = len(homes), homes[0].shape[0]
    rows = chunks * part
    result, losses = pl.pallas_call(
        unpack_kernel,
        out_shape=(
            jax.ShapeDtypeStruct((rows, width), BF),
            jax.ShapeDtypeStruct((rows // LANES, LANES), F32),
        ),
        in_specs=[VMEM] * chunks,
        out_specs=(ANY, VMEM),
        scratch_shapes=[pltpu.SemaphoreType.DMA((chunks,))],
        compiler_params=pltpu.CompilerParams(vmem_limit_bytes=SMALL_VMEM),
    )(*homes)
    return (result, losses.reshape(rows))


def on_device_chains(chunks, block, activations, targets, *weights):
    axes = ("coarse", "fine")
    devices = lax.axis_size(axes)
    rows, width = activations.shape
    part = rows // chunks
    each = part // devices
    near = FINE_HOP * each
    far = COARSE_HOP * lax.axis_size("fine") * each

    def spread(values):
        shaped = values.reshape((devices, each) + values.shape[1:])
        moved = lax.all_to_all(shaped, axes, 0, 0, tiled=True)
        return moved.reshape(values.shape)

    there = []
    pieces = [pack(activations, targets, chunks)]
    if chunks > 1:
        pieces += rest(activations, chunks)
    for piece in pieces:
        there.append(spread(piece))
    losses = None
    homes = []
    for chunk in range(chunks):
        grad, *losses = run_chains(
            there[0], there[chunk], *(losses or [None]), weights, near, far, block, chunk,
            chunk == chunks - 1,
        )
        homes.append(spread(grad))
    return unpack(homes, width)


def chains_fit(mesh, rows, chunks, block):
    devices = mesh.shape["coarse"] * mesh.shape["fine"]
    part = rows // chunks
    if rows % chunks or part % devices or part % block or part % LANES:
        return False
    each = part // devices
    far = COARSE_HOP * mesh.shape["fine"] * each
    near = FINE_HOP * each
    return near % 16 == 0 and far % 16 == 0 and chunks * PIECES <= LANES


def solution(mesh):
    in_specs = (
        P(("coarse", "fine"), None),
        P(("coarse", "fine")),
        P(),
        P(),
        P(),
        P(),
        P(),
        P(),
        P(),
    )
    out_specs = (P(("coarse", "fine"), None), P(("coarse", "fine")))

    def step(activations, *others):
        rows = activations.shape[0] // mesh.size
        chained = chains_fit(mesh, rows, CHUNKS, BLOCK)
        body = functools.partial(on_device_chains, CHUNKS, BLOCK) if chained else on_device

        spread = jax.shard_map(
            body, mesh=mesh, in_specs=in_specs, out_specs=out_specs, check_vma=False
        )
        return spread(activations, *others)

    return step
```

```python
import functools
import math

import jax
import jax.numpy as jnp
from jax import lax
from jax.experimental import pallas as pl
from jax.experimental.pallas import tpu as pltpu
from jax.sharding import PartitionSpec as P


COARSE_HOP = 4
FINE_HOP = 2
LANES = 128
PIECES = 3
CHUNKS = 2
BLOCK = 256
WHOLE_VMEM = 60 * 1024 * 1024
PACK_STEPS = 4
KERNEL_VMEM = 52500 << 10
SMALL_VMEM = 8 << 20


eps = 1e-05


def from_behind(value, axis, steps):
    count = lax.axis_size(axis)
    pairs = [(source, (source + steps) % count) for source in range(count)]
    return lax.ppermute(value, axis, pairs)


def norm_rows(values):
    average = jnp.mean(values, axis=-1, keepdims=True)
    centred = values - average
    factor = lax.rsqrt(jnp.mean(centred * centred, axis=-1, keepdims=True) + eps)
    return (centred * factor, factor)


def norm_back(normal, factor, upward):
    first_term = upward - jnp.mean(upward, axis=-1, keepdims=True)
    return (first_term - normal * jnp.mean(upward * normal, axis=-1, keepdims=True)) * factor


def gelu_exact(inputs):
    return 0.5 * inputs * (1.0 + lax.erf(inputs * (1.0 / math.sqrt(2.0))))


def gelu_slope(inputs):
    return 0.5 * (1.0 + lax.erf(inputs * (1.0 / math.sqrt(2.0)))) + inputs * jnp.exp(
        -0.5 * inputs * inputs
    ) * (1.0 / math.sqrt(2.0 * math.pi))


def product(leading, trailing):
    return jnp.dot(leading, trailing, preferred_element_type=jnp.float32)


def product_t(leading, trailing):
    return lax.dot_general(
        leading, trailing, (((1,), (1,)), ((), ())), preferred_element_type=jnp.float32
    )


def inner_pair(shard_rows):
    near_behind = from_behind(shard_rows, "fine", 2)
    near_ahead = from_behind(shard_rows, "fine", -2)
    far_behind = from_behind(near_behind, "coarse", 1)
    far_ahead = from_behind(near_ahead, "coarse", -1)
    fine_index = lax.axis_index("fine")
    fine_count = lax.axis_size("fine")
    behind_rows = jnp.where(fine_index < 2, far_behind, near_behind)
    ahead_rows = jnp.where(fine_index >= fine_count - 2, far_ahead, near_ahead)
    return (behind_rows, ahead_rows)


def outer_pair(shard_rows):
    behind_rows = from_behind(shard_rows, "coarse", COARSE_HOP)
    ahead_rows = from_behind(shard_rows, "coarse", -COARSE_HOP)
    return (behind_rows, ahead_rows)


def residual_block_forward(block_in, squeeze, taps, expand, neighbours):
    normal_in, _ = norm_rows(block_in.astype(jnp.float32))
    entry_act = gelu_exact(normal_in).astype(jnp.bfloat16)
    squeezed = product(entry_act, squeeze)
    normal_mid, _ = norm_rows(squeezed)
    middle = gelu_exact(normal_mid).astype(jnp.bfloat16)
    behind_rows, ahead_rows = neighbours(middle)
    conv_sum = (
        product(behind_rows, taps[0]) + product(middle, taps[1]) + product(ahead_rows, taps[2])
    )
    normal_conv, _ = norm_rows(conv_sum)
    closing = gelu_exact(normal_conv).astype(jnp.bfloat16)
    block_out = (block_in.astype(jnp.float32) + product(closing, expand)).astype(jnp.bfloat16)
    return (block_out, squeezed, conv_sum)


def residual_block_backward(
    block_in, squeezed, conv_sum, squeeze, taps, expand, neighbours, gradient_result
):
    dclosing = product_t(gradient_result.astype(jnp.bfloat16), expand)
    normal_conv, factor_conv = norm_rows(conv_sum)
    dconv = norm_back(normal_conv, factor_conv, gelu_slope(normal_conv) * dclosing).astype(
        jnp.bfloat16
    )
    behind_rows, ahead_rows = neighbours(dconv)
    dmiddle = (
        product_t(ahead_rows, taps[0]) + product_t(dconv, taps[1]) + product_t(behind_rows, taps[2])
    )
    normal_mid, factor_mid = norm_rows(squeezed)
    dsqueezed = norm_back(normal_mid, factor_mid, gelu_slope(normal_mid) * dmiddle).astype(
        jnp.bfloat16
    )
    dentry = product_t(dsqueezed, squeeze)
    normal_in, factor_in = norm_rows(block_in.astype(jnp.float32))
    return gradient_result + norm_back(normal_in, factor_in, gelu_slope(normal_in) * dentry)


def on_device(
    activations,
    targets,
    inner_squeeze_weight,
    inner_filter_taps,
    inner_expand_weight,
    outer_squeeze_weight,
    outer_filter_taps,
    outer_expand_weight,
    decoder,
):
    outer_block_input, inner_bottleneck_rows, inner_convolved = residual_block_forward(
        activations, inner_squeeze_weight, inner_filter_taps, inner_expand_weight, inner_pair
    )
    final_output, outer_bottleneck_rows, outer_convolved = residual_block_forward(
        outer_block_input, outer_squeeze_weight, outer_filter_taps, outer_expand_weight, outer_pair
    )
    normal_final, factor_final = norm_rows(final_output.astype(jnp.float32))
    normed = normal_final.astype(jnp.bfloat16)
    logits = product_t(normed, decoder)
    exponent = jnp.exp(logits)
    totals = jnp.sum(exponent, axis=-1, keepdims=True)
    classes = jnp.arange(decoder.shape[0], dtype=jnp.int32)
    onehot = (targets[:, None] == classes[None, :]).astype(jnp.float32)
    token_loss = jnp.log(totals[:, 0]) - jnp.sum(logits * onehot, axis=-1)
    dlogits = (32.0 * (exponent / totals - onehot)).astype(jnp.bfloat16)
    gradient_result = norm_back(normal_final, factor_final, product(dlogits, decoder))
    gradient_result = residual_block_backward(
        outer_block_input,
        outer_bottleneck_rows,
        outer_convolved,
        outer_squeeze_weight,
        outer_filter_taps,
        outer_expand_weight,
        outer_pair,
        gradient_result,
    )
    gradient_result = residual_block_backward(
        activations,
        inner_bottleneck_rows,
        inner_convolved,
        inner_squeeze_weight,
        inner_filter_taps,
        inner_expand_weight,
        inner_pair,
        gradient_result,
    )
    return (gradient_result.astype(jnp.bfloat16), token_loss)


BF = jnp.bfloat16
F32 = jnp.float32
ROOT_HALF = math.sqrt(0.5)
BELL = math.sqrt(2.0 / math.pi)


def scaled_norm(values, scale):
    average = jnp.mean(values, axis=-1, keepdims=True)
    centred = values - average
    factor = lax.rsqrt(jnp.mean(centred * centred, axis=-1, keepdims=True) + eps)
    return (centred * (factor * scale), factor)


def activate(values, kept, rows):
    scaled_ref, slope_ref, factor_ref = kept
    scaled, factor = scaled_norm(values, ROOT_HALF)
    half = ROOT_HALF * lax.erf(scaled) + ROOT_HALF
    scaled_ref[rows, :] = scaled
    slope_ref[rows, :] = half + scaled * (BELL * jnp.exp(-(scaled * scaled)))
    factor_ref[rows, :] = jnp.broadcast_to(factor, (factor.shape[0], LANES))
    return (scaled * half).astype(BF)


def back(upward, kept, rows):
    scaled_ref, slope_ref, factor_ref = kept
    scaled = scaled_ref[rows, :]
    through = slope_ref[rows, :] * upward
    mean = jnp.mean(through, axis=-1, keepdims=True)
    along = 2.0 * jnp.mean(through * scaled, axis=-1, keepdims=True)
    return (through - mean - scaled * along) * (factor_ref[rows, :][:, :1] * ROOT_HALF)


def chain_kernel(near, far, block, chunk, last, *refs):
    refs = list(refs)
    first_ref = refs.pop(0)
    x_ref = refs.pop(0) if chunk else first_ref
    before_ref = refs.pop(0) if chunk else None
    *weights_far, dec_ref = refs[:7]
    refs = refs[7:]
    grad_ref = refs.pop(0)
    loss_ref = None if last else refs.pop(0)
    ws_in, wt_in, we_in, ws_out, wt_out, we_out = refs[:6]
    dec_pad, mid_a, mid_b, outer_in, carried = refs[6:11]
    kept = [refs[start : start + 3] for start in range(11, 29, 3)]
    in_a, mid_kept_a, con_a, in_b, mid_kept_b, con_b = kept
    sems = refs[29]
    total, width = x_ref.shape[0], ws_in.shape[0]
    wide, classes = pl.ds(0, width), dec_ref.shape[0]
    starts = range(0, total, block)
    copies = [
        pltpu.make_async_copy(source, target, sems.at[index])
        for index, (source, target) in enumerate(zip(weights_far, refs[:6]))
    ]
    for copy in copies:
        copy.start()

    dec_pad[...] = jnp.zeros_like(dec_pad)
    dec_pad[pl.ds(0, classes), :] = dec_ref[...]

    def wrap(ref):
        ref[pl.ds(0, near), :] = ref[pl.ds(total, near), :]
        ref[pl.ds(total + near, near), :] = ref[pl.ds(near, near), :]

    def near_rows(ref, start, shift):
        return ref[pl.ds(start + near + shift, block), :]

    def far_rows(ref, start, shift):
        at = (start + shift) % total
        if at + block <= total:
            return ref[pl.ds(at, block), :]
        return jnp.concatenate([ref[at:total, :], ref[: at + block - total, :]])

    def conv(behind, here, ahead, taps):
        return product(
            jnp.concatenate([behind, here, ahead], axis=1), taps[...].reshape(-1, taps.shape[2])
        )

    meet = 2 * far % total == 0

    def both_ends(taps):
        return (taps[0].astype(F32) + taps[2].astype(F32)).astype(BF)

    def far_conv(behind, here, ahead, taps):
        if not meet:
            return conv(behind, here, ahead, taps)
        weight = jnp.concatenate([both_ends(taps), taps[1]])
        return product(jnp.concatenate([behind, here], axis=1), weight)

    def far_conv_back(behind, here, ahead, taps):
        if not meet:
            return conv_back(behind, here, ahead, taps)
        weight = jnp.concatenate([both_ends(taps), taps[1]], axis=1)
        return product_t(jnp.concatenate([ahead, here], axis=1), weight)

    def conv_back(behind, here, ahead, taps):
        return product_t(
            jnp.concatenate([ahead, here, behind], axis=1),
            jnp.concatenate([taps[0], taps[1], taps[2]], axis=1),
        )

    for start in starts:
        rows = pl.ds(start, block)
        entry = activate(x_ref[rows, wide].astype(F32), in_a, rows)
        if start == 0:
            copies[0].wait()
        middle = activate(product(entry, ws_in[...]), mid_kept_a, rows)
        mid_a[pl.ds(start + near, block), :] = middle
    wrap(mid_a)

    for copy in copies[1:4]:
        copy.wait()
    for start in starts:
        rows = pl.ds(start, block)
        shifted = [near_rows(mid_a, start, shift) for shift in (-near, 0, near)]
        closing = activate(conv(*shifted, wt_in), con_a, rows)
        following = (x_ref[rows, wide].astype(F32) + product(closing, we_in[...])).astype(BF)
        outer_in[rows, :] = following
        entry = activate(following.astype(F32), in_b, rows)
        mid_b[rows, :] = activate(product(entry, ws_out[...]), mid_kept_b, rows)

    for copy in copies[4:]:
        copy.wait()
    for start in starts:
        rows = pl.ds(start, block)
        shifted = [far_rows(mid_b, start, shift) for shift in (-far, 0, far)]
        closing = activate(far_conv(*shifted, wt_out), con_b, rows)
        final = (outer_in[rows, :].astype(F32) + product(closing, we_out[...])).astype(BF)
        normal, factor = scaled_norm(final.astype(F32), 1.0)
        logits = product_t(normal.astype(BF), dec_pad[...])
        lane = lax.broadcasted_iota(jnp.int32, logits.shape, 1)
        exponent = jnp.where(lane < classes, jnp.exp(logits), 0.0)
        totals = jnp.sum(exponent, axis=-1, keepdims=True)
        target = first_ref[rows, pl.ds(width, LANES)].astype(F32)[:, chunk : chunk + 1]
        onehot = jnp.where(lane.astype(F32) == target, 1.0, 0.0)
        loss = jnp.log(totals) - jnp.sum(logits * onehot, axis=-1, keepdims=True)
        pieces = before_ref[rows, :].astype(F32) if chunk else jnp.zeros_like(logits)
        for part in range(PIECES):
            piece = loss.astype(BF).astype(F32)
            pieces = jnp.where(lane == chunk * PIECES + part, piece, pieces)
            loss = loss - piece
        if last:
            grad_ref[rows, pl.ds(width, LANES)] = pieces.astype(BF)
        else:
            loss_ref[rows, :] = pieces.astype(BF)
        dlogits = (32.0 * (exponent / totals - onehot)).astype(BF)
        upward = norm_back(normal, factor, product(dlogits, dec_pad[...]))
        carried[rows, :] = upward
        dclosing = product_t(upward.astype(BF), we_out[...])
        mid_a[rows, :] = back(dclosing, con_b, rows).astype(BF)

    for start in starts:
        rows = pl.ds(start, block)
        shifted = [far_rows(mid_a, start, shift) for shift in (-far, 0, far)]
        dmiddle = far_conv_back(*shifted, wt_out)
        dsqueezed = back(dmiddle, mid_kept_b, rows).astype(BF)
        upward = carried[rows, :] + back(product_t(dsqueezed, ws_out[...]), in_b, rows)
        carried[rows, :] = upward
        dclosing = product_t(upward.astype(BF), we_in[...])
        mid_b[pl.ds(start + near, block), :] = back(dclosing, con_a, rows).astype(BF)
    wrap(mid_b)

    for start in starts:
        rows = pl.ds(start, block)
        shifted = [near_rows(mid_b, start, shift) for shift in (-near, 0, near)]
        dmiddle = conv_back(*shifted, wt_in)
        dsqueezed = back(dmiddle, mid_kept_a, rows).astype(BF)
        upward = carried[rows, :] + back(product_t(dsqueezed, ws_in[...]), in_a, rows)
        grad_ref[rows, wide] = upward.astype(BF)


VMEM = pl.BlockSpec(memory_space=pltpu.VMEM)
ANY = pl.BlockSpec(memory_space=pl.ANY)


def run_chains(first, rows, before, weights, near, far, block, chunk, last):
    count = first.shape[0]
    width, bottleneck = weights[0].shape
    padded = count + 2 * near
    tile = jax.ShapeDtypeStruct((count, LANES), BF)
    if last:
        out_shape = (jax.ShapeDtypeStruct((count, width + LANES), BF),)
    else:
        out_shape = (jax.ShapeDtypeStruct((count, width), BF), tile)

    def kept(size):
        return [
            pltpu.VMEM((count, size), F32),
            pltpu.VMEM((count, size), F32),
            pltpu.VMEM((count, LANES), F32),
        ]

    one_block = kept(width) + kept(bottleneck) + kept(bottleneck)
    operands = ((first, rows, before) if chunk else (first,)) + weights
    return pl.pallas_call(
        functools.partial(chain_kernel, near, far, block, chunk, last),
        out_shape=out_shape,
        in_specs=[VMEM] * (3 if chunk else 1) + [ANY] * 6 + [VMEM],
        out_specs=(VMEM,) * len(out_shape),
        scratch_shapes=[pltpu.VMEM(weight.shape, BF) for weight in weights[:6]]
        + [
            pltpu.VMEM((LANES, width), BF),
            pltpu.VMEM((padded, bottleneck), BF),
            pltpu.VMEM((padded, bottleneck), BF),
            pltpu.VMEM((count, width), BF),
            pltpu.VMEM((count, width), F32),
        ]
        + one_block
        + one_block
        + [pltpu.SemaphoreType.DMA((6,))],
        compiler_params=pltpu.CompilerParams(vmem_limit_bytes=KERNEL_VMEM),
        cost_estimate=pl.CostEstimate(
            flops=count * 36 * width * bottleneck, bytes_accessed=24 << 20, transcendentals=0
        ),
    )(*operands)


def pack_kernel(chunks, x_ref, target_ref, out_ref, buffer, in_sems, out_sems):
    part, width = buffer.shape[0], x_ref.shape[1]
    size = part // PACK_STEPS
    arrivals, departures = [], []
    for step in range(PACK_STEPS):
        rows = pl.ds(step * size, size)
        here = buffer.at[rows, pl.ds(0, width)]
        arrivals.append(pltpu.make_async_copy(x_ref.at[rows, :], here, in_sems.at[step]))
        departures.append(
            pltpu.make_async_copy(buffer.at[rows, :], out_ref.at[rows, :], out_sems.at[step])
        )
        arrivals[-1].start()
    lane = lax.broadcasted_iota(jnp.int32, (LANES, LANES), 1)
    for start in range(0, part, LANES):
        tile = jnp.zeros((LANES, LANES), F32)
        for chunk in range(chunks):
            row = target_ref[pl.ds((chunk * part + start) // LANES, 1), :].astype(F32)
            column = jnp.transpose(jnp.broadcast_to(row, (LANES, LANES)))
            tile = jnp.where(lane == chunk, column, tile)
        buffer[pl.ds(start, LANES), pl.ds(width, LANES)] = tile.astype(BF)
    for arrival, departure in zip(arrivals, departures):
        arrival.wait()
        departure.start()
    for departure in departures:
        departure.wait()


def pack(activations, targets, chunks):
    rows, width = activations.shape
    shape = (rows // chunks, width + LANES)
    return pl.pallas_call(
        functools.partial(pack_kernel, chunks),
        out_shape=jax.ShapeDtypeStruct(shape, BF),
        in_specs=[ANY, VMEM],
        out_specs=ANY,
        scratch_shapes=[
            pltpu.VMEM(shape, BF),
            pltpu.SemaphoreType.DMA((PACK_STEPS,)),
            pltpu.SemaphoreType.DMA((PACK_STEPS,)),
        ],
        compiler_params=pltpu.CompilerParams(vmem_limit_bytes=WHOLE_VMEM),
    )(activations, targets.reshape(rows // LANES, LANES))


def rest_kernel(x_ref, *refs):
    outs, sems = refs[:-1], refs[-1]
    part = outs[0].shape[0]
    copies = [
        pltpu.make_async_copy(x_ref.at[pl.ds((chunk + 1) * part, part), :], out, sems.at[chunk])
        for chunk, out in enumerate(outs)
    ]
    for copy in copies:
        copy.start()
    for copy in copies:
        copy.wait()


def rest(activations, chunks):
    rows, width = activations.shape
    return pl.pallas_call(
        rest_kernel,
        out_shape=(jax.ShapeDtypeStruct((rows // chunks, width), BF),) * (chunks - 1),
        in_specs=[ANY],
        out_specs=(VMEM,) * (chunks - 1),
        scratch_shapes=[pltpu.SemaphoreType.DMA((chunks - 1,))],
        compiler_params=pltpu.CompilerParams(vmem_limit_bytes=WHOLE_VMEM),
    )(activations)


def unpack_kernel(*refs):
    *pieces, out_ref, loss_ref, sems = refs
    part, width = pieces[-1].shape[0], out_ref.shape[1]
    copies = []
    for chunk, piece in enumerate(pieces):
        place = out_ref.at[pl.ds(chunk * part, part), :]
        copies.append(pltpu.make_async_copy(piece.at[:, pl.ds(0, width)], place, sems.at[chunk]))
        copies[-1].start()
    for start in range(0, part, LANES):
        tile = pieces[-1][pl.ds(start, LANES), pl.ds(width, LANES)].astype(F32)
        flat = jnp.transpose(tile)
        for chunk in range(len(pieces)):
            lines = [flat[chunk * PIECES + part : chunk * PIECES + part + 1] for part in range(PIECES)]
            loss_ref[pl.ds((chunk * pieces[-1].shape[0] + start) // LANES, 1), :] = sum(
                lines[1:], lines[0]
            )
    for copy in copies:
        copy.wait()


def unpack(homes, width):
    chunks, part = len(homes), homes[0].shape[0]
    rows = chunks * part
    result, losses = pl.pallas_call(
        unpack_kernel,
        out_shape=(
            jax.ShapeDtypeStruct((rows, width), BF),
            jax.ShapeDtypeStruct((rows // LANES, LANES), F32),
        ),
        in_specs=[VMEM] * chunks,
        out_specs=(ANY, VMEM),
        scratch_shapes=[pltpu.SemaphoreType.DMA((chunks,))],
        compiler_params=pltpu.CompilerParams(vmem_limit_bytes=SMALL_VMEM),
    )(*homes)
    return (result, losses.reshape(rows))


def on_device_chains(chunks, block, activations, targets, *weights):
    axes = ("coarse", "fine")
    devices = lax.axis_size(axes)
    rows, width = activations.shape
    part = rows // chunks
    each = part // devices
    near = FINE_HOP * each
    far = COARSE_HOP * lax.axis_size("fine") * each

    def spread(values):
        shaped = values.reshape((devices, each) + values.shape[1:])
        moved = lax.all_to_all(shaped, axes, 0, 0, tiled=True)
        return moved.reshape(values.shape)

    there = []
    pieces = [pack(activations, targets, chunks)]
    if chunks > 1:
        pieces += rest(activations, chunks)
    for piece in pieces:
        there.append(spread(piece))
    losses = None
    homes = []
    for chunk in range(chunks):
        grad, *losses = run_chains(
            there[0], there[chunk], *(losses or [None]), weights, near, far, block, chunk,
            chunk == chunks - 1,
        )
        homes.append(spread(grad))
    return unpack(homes, width)


def chains_fit(mesh, rows, chunks, block):
    devices = mesh.shape["coarse"] * mesh.shape["fine"]
    part = rows // chunks
    if rows % chunks or part % devices or part % block or part % LANES:
        return False
    each = part // devices
    far = COARSE_HOP * mesh.shape["fine"] * each
    near = FINE_HOP * each
    return near % 16 == 0 and far % 16 == 0 and chunks * PIECES <= LANES


def solution(mesh):
    in_specs = (
        P(("coarse", "fine"), None),
        P(("coarse", "fine")),
        P(),
        P(),
        P(),
        P(),
        P(),
        P(),
        P(),
    )
    out_specs = (P(("coarse", "fine"), None), P(("coarse", "fine")))

    def step(activations, *others):
        rows = activations.shape[0] // mesh.size
        chained = chains_fit(mesh, rows, CHUNKS, BLOCK)
        body = functools.partial(on_device_chains, CHUNKS, BLOCK) if chained else on_device

        spread = jax.shard_map(
            body, mesh=mesh, in_specs=in_specs, out_specs=out_specs, check_vma=False
        )
        return spread(activations, *others)

    return step
```

```python
import functools
import math

import jax
import jax.numpy as jnp
from jax import lax
from jax.experimental import pallas as pl
from jax.experimental.pallas import tpu as pltpu
from jax.sharding import PartitionSpec as P


COARSE_HOP = 4
FINE_HOP = 2
LANES = 128
PIECES = 3
CHUNKS = 2
BLOCK = 256
WHOLE_VMEM = 60 * 1024 * 1024
PACK_STEPS = 4
KERNEL_VMEM = 52500 << 10
SMALL_VMEM = 8 << 20


eps = 1e-05


def from_behind(value, axis, steps):
    count = lax.axis_size(axis)
    pairs = [(source, (source + steps) % count) for source in range(count)]
    return lax.ppermute(value, axis, pairs)


def norm_rows(values):
    average = jnp.mean(values, axis=-1, keepdims=True)
    centred = values - average
    factor = lax.rsqrt(jnp.mean(centred * centred, axis=-1, keepdims=True) + eps)
    return (centred * factor, factor)


def norm_back(normal, factor, upward):
    first_term = upward - jnp.mean(upward, axis=-1, keepdims=True)
    return (first_term - normal * jnp.mean(upward * normal, axis=-1, keepdims=True)) * factor


def gelu_exact(inputs):
    return 0.5 * inputs * (1.0 + lax.erf(inputs * (1.0 / math.sqrt(2.0))))


def gelu_slope(inputs):
    return 0.5 * (1.0 + lax.erf(inputs * (1.0 / math.sqrt(2.0)))) + inputs * jnp.exp(
        -0.5 * inputs * inputs
    ) * (1.0 / math.sqrt(2.0 * math.pi))


def product(leading, trailing):
    return jnp.dot(leading, trailing, preferred_element_type=jnp.float32)


def product_t(leading, trailing):
    return lax.dot_general(
        leading, trailing, (((1,), (1,)), ((), ())), preferred_element_type=jnp.float32
    )


def inner_pair(shard_rows):
    near_behind = from_behind(shard_rows, "fine", 2)
    near_ahead = from_behind(shard_rows, "fine", -2)
    far_behind = from_behind(near_behind, "coarse", 1)
    far_ahead = from_behind(near_ahead, "coarse", -1)
    fine_index = lax.axis_index("fine")
    fine_count = lax.axis_size("fine")
    behind_rows = jnp.where(fine_index < 2, far_behind, near_behind)
    ahead_rows = jnp.where(fine_index >= fine_count - 2, far_ahead, near_ahead)
    return (behind_rows, ahead_rows)


def outer_pair(shard_rows):
    behind_rows = from_behind(shard_rows, "coarse", COARSE_HOP)
    ahead_rows = from_behind(shard_rows, "coarse", -COARSE_HOP)
    return (behind_rows, ahead_rows)


def residual_block_forward(block_in, squeeze, taps, expand, neighbours):
    normal_in, _ = norm_rows(block_in.astype(jnp.float32))
    entry_act = gelu_exact(normal_in).astype(jnp.bfloat16)
    squeezed = product(entry_act, squeeze)
    normal_mid, _ = norm_rows(squeezed)
    middle = gelu_exact(normal_mid).astype(jnp.bfloat16)
    behind_rows, ahead_rows = neighbours(middle)
    conv_sum = (
        product(behind_rows, taps[0]) + product(middle, taps[1]) + product(ahead_rows, taps[2])
    )
    normal_conv, _ = norm_rows(conv_sum)
    closing = gelu_exact(normal_conv).astype(jnp.bfloat16)
    block_out = (block_in.astype(jnp.float32) + product(closing, expand)).astype(jnp.bfloat16)
    return (block_out, squeezed, conv_sum)


def residual_block_backward(
    block_in, squeezed, conv_sum, squeeze, taps, expand, neighbours, gradient_result
):
    dclosing = product_t(gradient_result.astype(jnp.bfloat16), expand)
    normal_conv, factor_conv = norm_rows(conv_sum)
    dconv = norm_back(normal_conv, factor_conv, gelu_slope(normal_conv) * dclosing).astype(
        jnp.bfloat16
    )
    behind_rows, ahead_rows = neighbours(dconv)
    dmiddle = (
        product_t(ahead_rows, taps[0]) + product_t(dconv, taps[1]) + product_t(behind_rows, taps[2])
    )
    normal_mid, factor_mid = norm_rows(squeezed)
    dsqueezed = norm_back(normal_mid, factor_mid, gelu_slope(normal_mid) * dmiddle).astype(
        jnp.bfloat16
    )
    dentry = product_t(dsqueezed, squeeze)
    normal_in, factor_in = norm_rows(block_in.astype(jnp.float32))
    return gradient_result + norm_back(normal_in, factor_in, gelu_slope(normal_in) * dentry)


def on_device(
    activations,
    targets,
    inner_squeeze_weight,
    inner_filter_taps,
    inner_expand_weight,
    outer_squeeze_weight,
    outer_filter_taps,
    outer_expand_weight,
    decoder,
):
    outer_block_input, inner_bottleneck_rows, inner_convolved = residual_block_forward(
        activations, inner_squeeze_weight, inner_filter_taps, inner_expand_weight, inner_pair
    )
    final_output, outer_bottleneck_rows, outer_convolved = residual_block_forward(
        outer_block_input, outer_squeeze_weight, outer_filter_taps, outer_expand_weight, outer_pair
    )
    normal_final, factor_final = norm_rows(final_output.astype(jnp.float32))
    normed = normal_final.astype(jnp.bfloat16)
    logits = product_t(normed, decoder)
    exponent = jnp.exp(logits)
    totals = jnp.sum(exponent, axis=-1, keepdims=True)
    classes = jnp.arange(decoder.shape[0], dtype=jnp.int32)
    onehot = (targets[:, None] == classes[None, :]).astype(jnp.float32)
    token_loss = jnp.log(totals[:, 0]) - jnp.sum(logits * onehot, axis=-1)
    dlogits = (32.0 * (exponent / totals - onehot)).astype(jnp.bfloat16)
    gradient_result = norm_back(normal_final, factor_final, product(dlogits, decoder))
    gradient_result = residual_block_backward(
        outer_block_input,
        outer_bottleneck_rows,
        outer_convolved,
        outer_squeeze_weight,
        outer_filter_taps,
        outer_expand_weight,
        outer_pair,
        gradient_result,
    )
    gradient_result = residual_block_backward(
        activations,
        inner_bottleneck_rows,
        inner_convolved,
        inner_squeeze_weight,
        inner_filter_taps,
        inner_expand_weight,
        inner_pair,
        gradient_result,
    )
    return (gradient_result.astype(jnp.bfloat16), token_loss)


BF = jnp.bfloat16
F32 = jnp.float32
ROOT_HALF = math.sqrt(0.5)
BELL = math.sqrt(2.0 / math.pi)


def scaled_norm(values, scale):
    average = jnp.mean(values, axis=-1, keepdims=True)
    centred = values - average
    factor = lax.rsqrt(jnp.mean(centred * centred, axis=-1, keepdims=True) + eps)
    return (centred * (factor * scale), factor)


def activate(values, kept, rows):
    scaled_ref, slope_ref, factor_ref = kept
    scaled, factor = scaled_norm(values, ROOT_HALF)
    half = ROOT_HALF * lax.erf(scaled) + ROOT_HALF
    scaled_ref[rows, :] = scaled
    slope_ref[rows, :] = half + scaled * (BELL * jnp.exp(-(scaled * scaled)))
    factor_ref[rows, :] = jnp.broadcast_to(factor, (factor.shape[0], LANES))
    return (scaled * half).astype(BF)


def back(upward, kept, rows):
    scaled_ref, slope_ref, factor_ref = kept
    scaled = scaled_ref[rows, :]
    through = slope_ref[rows, :] * upward
    mean = jnp.mean(through, axis=-1, keepdims=True)
    along = 2.0 * jnp.mean(through * scaled, axis=-1, keepdims=True)
    return (through - mean - scaled * along) * (factor_ref[rows, :][:, :1] * ROOT_HALF)


def chain_kernel(near, far, block, chunk, last, *refs):
    refs = list(refs)
    first_ref = refs.pop(0)
    x_ref = refs.pop(0) if chunk else first_ref
    before_ref = refs.pop(0) if chunk else None
    *weights_far, dec_ref = refs[:7]
    refs = refs[7:]
    grad_ref = refs.pop(0)
    loss_ref = None if last else refs.pop(0)
    ws_in, wt_in, we_in, ws_out, wt_out, we_out = refs[:6]
    dec_pad, mid_a, mid_b, outer_in, carried = refs[6:11]
    kept = [refs[start : start + 3] for start in range(11, 29, 3)]
    in_a, mid_kept_a, con_a, in_b, mid_kept_b, con_b = kept
    sems = refs[29]
    total, width = x_ref.shape[0], ws_in.shape[0]
    wide, classes = pl.ds(0, width), dec_ref.shape[0]
    starts = range(0, total, block)
    copies = [
        pltpu.make_async_copy(source, target, sems.at[index])
        for index, (source, target) in enumerate(zip(weights_far, refs[:6]))
    ]
    for copy in copies:
        copy.start()

    dec_pad[...] = jnp.zeros_like(dec_pad)
    dec_pad[pl.ds(0, classes), :] = dec_ref[...]

    def wrap(ref):
        ref[pl.ds(0, near), :] = ref[pl.ds(total, near), :]
        ref[pl.ds(total + near, near), :] = ref[pl.ds(near, near), :]

    def near_rows(ref, start, shift):
        return ref[pl.ds(start + near + shift, block), :]

    def far_rows(ref, start, shift):
        at = (start + shift) % total
        if at + block <= total:
            return ref[pl.ds(at, block), :]
        return jnp.concatenate([ref[at:total, :], ref[: at + block - total, :]])

    def conv(behind, here, ahead, taps):
        return product(
            jnp.concatenate([behind, here, ahead], axis=1), taps[...].reshape(-1, taps.shape[2])
        )

    meet = 2 * far % total == 0

    def both_ends(taps):
        return (taps[0].astype(F32) + taps[2].astype(F32)).astype(BF)

    def far_conv(behind, here, ahead, taps):
        if not meet:
            return conv(behind, here, ahead, taps)
        weight = jnp.concatenate([both_ends(taps), taps[1]])
        return product(jnp.concatenate([behind, here], axis=1), weight)

    def far_conv_back(behind, here, ahead, taps):
        if not meet:
            return conv_back(behind, here, ahead, taps)
        weight = jnp.concatenate([both_ends(taps), taps[1]], axis=1)
        return product_t(jnp.concatenate([ahead, here], axis=1), weight)

    def conv_back(behind, here, ahead, taps):
        return product_t(
            jnp.concatenate([ahead, here, behind], axis=1),
            jnp.concatenate([taps[0], taps[1], taps[2]], axis=1),
        )

    for start in starts:
        rows = pl.ds(start, block)
        entry = activate(x_ref[rows, wide].astype(F32), in_a, rows)
        if start == 0:
            copies[0].wait()
        middle = activate(product(entry, ws_in[...]), mid_kept_a, rows)
        mid_a[pl.ds(start + near, block), :] = middle
    wrap(mid_a)

    for copy in copies[1:4]:
        copy.wait()
    for start in starts:
        rows = pl.ds(start, block)
        shifted = [near_rows(mid_a, start, shift) for shift in (-near, 0, near)]
        closing = activate(conv(*shifted, wt_in), con_a, rows)
        following = (x_ref[rows, wide].astype(F32) + product(closing, we_in[...])).astype(BF)
        outer_in[rows, :] = following
        entry = activate(following.astype(F32), in_b, rows)
        mid_b[rows, :] = activate(product(entry, ws_out[...]), mid_kept_b, rows)

    for copy in copies[4:]:
        copy.wait()
    for start in starts:
        rows = pl.ds(start, block)
        shifted = [far_rows(mid_b, start, shift) for shift in (-far, 0, far)]
        closing = activate(far_conv(*shifted, wt_out), con_b, rows)
        final = (outer_in[rows, :].astype(F32) + product(closing, we_out[...])).astype(BF)
        normal, factor = scaled_norm(final.astype(F32), 1.0)
        logits = product_t(normal.astype(BF), dec_pad[...])
        lane = lax.broadcasted_iota(jnp.int32, logits.shape, 1)
        exponent = jnp.where(lane < classes, jnp.exp(logits), 0.0)
        totals = jnp.sum(exponent, axis=-1, keepdims=True)
        target = first_ref[rows, pl.ds(width, LANES)].astype(F32)[:, chunk : chunk + 1]
        onehot = jnp.where(lane.astype(F32) == target, 1.0, 0.0)
        loss = jnp.log(totals) - jnp.sum(logits * onehot, axis=-1, keepdims=True)
        pieces = before_ref[rows, :].astype(F32) if chunk else jnp.zeros_like(logits)
        for part in range(PIECES):
            piece = loss.astype(BF).astype(F32)
            pieces = jnp.where(lane == chunk * PIECES + part, piece, pieces)
            loss = loss - piece
        if last:
            grad_ref[rows, pl.ds(width, LANES)] = pieces.astype(BF)
        else:
            loss_ref[rows, :] = pieces.astype(BF)
        dlogits = (32.0 * (exponent / totals - onehot)).astype(BF)
        upward = norm_back(normal, factor, product(dlogits, dec_pad[...]))
        carried[rows, :] = upward
        dclosing = product_t(upward.astype(BF), we_out[...])
        mid_a[rows, :] = back(dclosing, con_b, rows).astype(BF)

    for start in starts:
        rows = pl.ds(start, block)
        shifted = [far_rows(mid_a, start, shift) for shift in (-far, 0, far)]
        dmiddle = far_conv_back(*shifted, wt_out)
        dsqueezed = back(dmiddle, mid_kept_b, rows).astype(BF)
        upward = carried[rows, :] + back(product_t(dsqueezed, ws_out[...]), in_b, rows)
        carried[rows, :] = upward
        dclosing = product_t(upward.astype(BF), we_in[...])
        mid_b[pl.ds(start + near, block), :] = back(dclosing, con_a, rows).astype(BF)
    wrap(mid_b)

    for start in starts:
        rows = pl.ds(start, block)
        shifted = [near_rows(mid_b, start, shift) for shift in (-near, 0, near)]
        dmiddle = conv_back(*shifted, wt_in)
        dsqueezed = back(dmiddle, mid_kept_a, rows).astype(BF)
        upward = carried[rows, :] + back(product_t(dsqueezed, ws_in[...]), in_a, rows)
        grad_ref[rows, wide] = upward.astype(BF)


VMEM = pl.BlockSpec(memory_space=pltpu.VMEM)
ANY = pl.BlockSpec(memory_space=pl.ANY)


def run_chains(first, rows, before, weights, near, far, block, chunk, last):
    count = first.shape[0]
    width, bottleneck = weights[0].shape
    padded = count + 2 * near
    tile = jax.ShapeDtypeStruct((count, LANES), BF)
    if last:
        out_shape = (jax.ShapeDtypeStruct((count, width + LANES), BF),)
    else:
        out_shape = (jax.ShapeDtypeStruct((count, width), BF), tile)

    def kept(size):
        return [
            pltpu.VMEM((count, size), F32),
            pltpu.VMEM((count, size), F32),
            pltpu.VMEM((count, LANES), F32),
        ]

    one_block = kept(width) + kept(bottleneck) + kept(bottleneck)
    operands = ((first, rows, before) if chunk else (first,)) + weights
    return pl.pallas_call(
        functools.partial(chain_kernel, near, far, block, chunk, last),
        out_shape=out_shape,
        in_specs=[VMEM] * (3 if chunk else 1) + [ANY] * 6 + [VMEM],
        out_specs=(VMEM,) * len(out_shape),
        scratch_shapes=[pltpu.VMEM(weight.shape, BF) for weight in weights[:6]]
        + [
            pltpu.VMEM((LANES, width), BF),
            pltpu.VMEM((padded, bottleneck), BF),
            pltpu.VMEM((padded, bottleneck), BF),
            pltpu.VMEM((count, width), BF),
            pltpu.VMEM((count, width), F32),
        ]
        + one_block
        + one_block
        + [pltpu.SemaphoreType.DMA((6,))],
        compiler_params=pltpu.CompilerParams(vmem_limit_bytes=KERNEL_VMEM),
        cost_estimate=pl.CostEstimate(
            flops=count * 36 * width * bottleneck, bytes_accessed=24 << 20, transcendentals=0
        ),
    )(*operands)


def pack_kernel(chunks, x_ref, target_far, out_ref, target_ref, buffer, in_sems, out_sems):
    target_copy = pltpu.make_async_copy(target_far, target_ref, in_sems.at[PACK_STEPS])
    target_copy.start()
    part, width = buffer.shape[0], x_ref.shape[1]
    size = part // PACK_STEPS
    arrivals, departures = [], []
    for step in range(PACK_STEPS):
        rows = pl.ds(step * size, size)
        here = buffer.at[rows, pl.ds(0, width)]
        arrivals.append(pltpu.make_async_copy(x_ref.at[rows, :], here, in_sems.at[step]))
        departures.append(
            pltpu.make_async_copy(buffer.at[rows, :], out_ref.at[rows, :], out_sems.at[step])
        )
        arrivals[-1].start()
    target_copy.wait()
    lane = lax.broadcasted_iota(jnp.int32, (LANES, LANES), 1)
    for start in range(0, part, LANES):
        tile = jnp.zeros((LANES, LANES), F32)
        for chunk in range(chunks):
            row = target_ref[pl.ds((chunk * part + start) // LANES, 1), :].astype(F32)
            column = jnp.transpose(jnp.broadcast_to(row, (LANES, LANES)))
            tile = jnp.where(lane == chunk, column, tile)
        buffer[pl.ds(start, LANES), pl.ds(width, LANES)] = tile.astype(BF)
    for arrival, departure in zip(arrivals, departures):
        arrival.wait()
        departure.start()
    for departure in departures:
        departure.wait()


def pack(activations, targets, chunks):
    rows, width = activations.shape
    shape = (rows // chunks, width + LANES)
    return pl.pallas_call(
        functools.partial(pack_kernel, chunks),
        out_shape=jax.ShapeDtypeStruct(shape, BF),
        in_specs=[ANY, ANY],
        out_specs=ANY,
        scratch_shapes=[
            pltpu.VMEM((rows // LANES, LANES), targets.dtype),
            pltpu.VMEM(shape, BF),
            pltpu.SemaphoreType.DMA((PACK_STEPS + 1,)),
            pltpu.SemaphoreType.DMA((PACK_STEPS,)),
        ],
        compiler_params=pltpu.CompilerParams(vmem_limit_bytes=WHOLE_VMEM),
    )(activations, targets.reshape(rows // LANES, LANES))


def rest_kernel(x_ref, *refs):
    outs, sems = refs[:-1], refs[-1]
    part = outs[0].shape[0]
    copies = [
        pltpu.make_async_copy(x_ref.at[pl.ds((chunk + 1) * part, part), :], out, sems.at[chunk])
        for chunk, out in enumerate(outs)
    ]
    for copy in copies:
        copy.start()
    for copy in copies:
        copy.wait()


def rest(activations, chunks):
    rows, width = activations.shape
    return pl.pallas_call(
        rest_kernel,
        out_shape=(jax.ShapeDtypeStruct((rows // chunks, width), BF),) * (chunks - 1),
        in_specs=[ANY],
        out_specs=(VMEM,) * (chunks - 1),
        scratch_shapes=[pltpu.SemaphoreType.DMA((chunks - 1,))],
        compiler_params=pltpu.CompilerParams(vmem_limit_bytes=WHOLE_VMEM),
    )(activations)


def unpack_kernel(*refs):
    *pieces, out_ref, loss_ref, sems = refs
    part, width = pieces[-1].shape[0], out_ref.shape[1]
    copies = []
    for chunk, piece in enumerate(pieces):
        place = out_ref.at[pl.ds(chunk * part, part), :]
        copies.append(pltpu.make_async_copy(piece.at[:, pl.ds(0, width)], place, sems.at[chunk]))
        copies[-1].start()
    for start in range(0, part, LANES):
        tile = pieces[-1][pl.ds(start, LANES), pl.ds(width, LANES)].astype(F32)
        flat = jnp.transpose(tile)
        for chunk in range(len(pieces)):
            lines = [flat[chunk * PIECES + part : chunk * PIECES + part + 1] for part in range(PIECES)]
            loss_ref[pl.ds((chunk * pieces[-1].shape[0] + start) // LANES, 1), :] = sum(
                lines[1:], lines[0]
            )
    for copy in copies:
        copy.wait()


def unpack(homes, width):
    chunks, part = len(homes), homes[0].shape[0]
    rows = chunks * part
    result, losses = pl.pallas_call(
        unpack_kernel,
        out_shape=(
            jax.ShapeDtypeStruct((rows, width), BF),
            jax.ShapeDtypeStruct((rows // LANES, LANES), F32),
        ),
        in_specs=[VMEM] * chunks,
        out_specs=(ANY, VMEM),
        scratch_shapes=[pltpu.SemaphoreType.DMA((chunks,))],
        compiler_params=pltpu.CompilerParams(vmem_limit_bytes=SMALL_VMEM),
    )(*homes)
    return (result, losses.reshape(rows))


def on_device_chains(chunks, block, activations, targets, *weights):
    axes = ("coarse", "fine")
    devices = lax.axis_size(axes)
    rows, width = activations.shape
    part = rows // chunks
    each = part // devices
    near = FINE_HOP * each
    far = COARSE_HOP * lax.axis_size("fine") * each

    def spread(values):
        shaped = values.reshape((devices, each) + values.shape[1:])
        moved = lax.all_to_all(shaped, axes, 0, 0, tiled=True)
        return moved.reshape(values.shape)

    there = []
    pieces = [pack(activations, targets, chunks)]
    if chunks > 1:
        pieces += rest(activations, chunks)
    for piece in pieces:
        there.append(spread(piece))
    losses = None
    homes = []
    for chunk in range(chunks):
        grad, *losses = run_chains(
            there[0], there[chunk], *(losses or [None]), weights, near, far, block, chunk,
            chunk == chunks - 1,
        )
        homes.append(spread(grad))
    return unpack(homes, width)


def chains_fit(mesh, rows, chunks, block):
    devices = mesh.shape["coarse"] * mesh.shape["fine"]
    part = rows // chunks
    if rows % chunks or part % devices or part % block or part % LANES:
        return False
    each = part // devices
    far = COARSE_HOP * mesh.shape["fine"] * each
    near = FINE_HOP * each
    return near % 16 == 0 and far % 16 == 0 and chunks * PIECES <= LANES


def solution(mesh):
    in_specs = (
        P(("coarse", "fine"), None),
        P(("coarse", "fine")),
        P(),
        P(),
        P(),
        P(),
        P(),
        P(),
        P(),
    )
    out_specs = (P(("coarse", "fine"), None), P(("coarse", "fine")))

    def step(activations, *others):
        rows = activations.shape[0] // mesh.size
        chained = chains_fit(mesh, rows, CHUNKS, BLOCK)
        body = functools.partial(on_device_chains, CHUNKS, BLOCK) if chained else on_device

        spread = jax.shard_map(
            body, mesh=mesh, in_specs=in_specs, out_specs=out_specs, check_vma=False
        )
        return spread(activations, *others)

    return step
```

```python
import functools
import math

import jax
import jax.numpy as jnp
from jax import lax
from jax.experimental import pallas as pl
from jax.experimental.pallas import tpu as pltpu
from jax.sharding import PartitionSpec as P


COARSE_HOP = 4
FINE_HOP = 2
LANES = 128
PIECES = 3
CHUNKS = 2
BLOCK = 256
WHOLE_VMEM = 60 * 1024 * 1024
PACK_STEPS = 4
KERNEL_VMEM = 52500 << 10
SMALL_VMEM = 8 << 20


eps = 1e-05


def from_behind(value, axis, steps):
    count = lax.axis_size(axis)
    pairs = [(source, (source + steps) % count) for source in range(count)]
    return lax.ppermute(value, axis, pairs)


def norm_rows(values):
    average = jnp.mean(values, axis=-1, keepdims=True)
    centred = values - average
    factor = lax.rsqrt(jnp.mean(centred * centred, axis=-1, keepdims=True) + eps)
    return (centred * factor, factor)


def norm_back(normal, factor, upward):
    first_term = upward - jnp.mean(upward, axis=-1, keepdims=True)
    return (first_term - normal * jnp.mean(upward * normal, axis=-1, keepdims=True)) * factor


def gelu_exact(inputs):
    return 0.5 * inputs * (1.0 + lax.erf(inputs * (1.0 / math.sqrt(2.0))))


def gelu_slope(inputs):
    return 0.5 * (1.0 + lax.erf(inputs * (1.0 / math.sqrt(2.0)))) + inputs * jnp.exp(
        -0.5 * inputs * inputs
    ) * (1.0 / math.sqrt(2.0 * math.pi))


def product(leading, trailing):
    return jnp.dot(leading, trailing, preferred_element_type=jnp.float32)


def product_t(leading, trailing):
    return lax.dot_general(
        leading, trailing, (((1,), (1,)), ((), ())), preferred_element_type=jnp.float32
    )


def inner_pair(shard_rows):
    near_behind = from_behind(shard_rows, "fine", 2)
    near_ahead = from_behind(shard_rows, "fine", -2)
    far_behind = from_behind(near_behind, "coarse", 1)
    far_ahead = from_behind(near_ahead, "coarse", -1)
    fine_index = lax.axis_index("fine")
    fine_count = lax.axis_size("fine")
    behind_rows = jnp.where(fine_index < 2, far_behind, near_behind)
    ahead_rows = jnp.where(fine_index >= fine_count - 2, far_ahead, near_ahead)
    return (behind_rows, ahead_rows)


def outer_pair(shard_rows):
    behind_rows = from_behind(shard_rows, "coarse", COARSE_HOP)
    ahead_rows = from_behind(shard_rows, "coarse", -COARSE_HOP)
    return (behind_rows, ahead_rows)


def residual_block_forward(block_in, squeeze, taps, expand, neighbours):
    normal_in, _ = norm_rows(block_in.astype(jnp.float32))
    entry_act = gelu_exact(normal_in).astype(jnp.bfloat16)
    squeezed = product(entry_act, squeeze)
    normal_mid, _ = norm_rows(squeezed)
    middle = gelu_exact(normal_mid).astype(jnp.bfloat16)
    behind_rows, ahead_rows = neighbours(middle)
    conv_sum = (
        product(behind_rows, taps[0]) + product(middle, taps[1]) + product(ahead_rows, taps[2])
    )
    normal_conv, _ = norm_rows(conv_sum)
    closing = gelu_exact(normal_conv).astype(jnp.bfloat16)
    block_out = (block_in.astype(jnp.float32) + product(closing, expand)).astype(jnp.bfloat16)
    return (block_out, squeezed, conv_sum)


def residual_block_backward(
    block_in, squeezed, conv_sum, squeeze, taps, expand, neighbours, gradient_result
):
    dclosing = product_t(gradient_result.astype(jnp.bfloat16), expand)
    normal_conv, factor_conv = norm_rows(conv_sum)
    dconv = norm_back(normal_conv, factor_conv, gelu_slope(normal_conv) * dclosing).astype(
        jnp.bfloat16
    )
    behind_rows, ahead_rows = neighbours(dconv)
    dmiddle = (
        product_t(ahead_rows, taps[0]) + product_t(dconv, taps[1]) + product_t(behind_rows, taps[2])
    )
    normal_mid, factor_mid = norm_rows(squeezed)
    dsqueezed = norm_back(normal_mid, factor_mid, gelu_slope(normal_mid) * dmiddle).astype(
        jnp.bfloat16
    )
    dentry = product_t(dsqueezed, squeeze)
    normal_in, factor_in = norm_rows(block_in.astype(jnp.float32))
    return gradient_result + norm_back(normal_in, factor_in, gelu_slope(normal_in) * dentry)


def on_device(
    activations,
    targets,
    inner_squeeze_weight,
    inner_filter_taps,
    inner_expand_weight,
    outer_squeeze_weight,
    outer_filter_taps,
    outer_expand_weight,
    decoder,
):
    outer_block_input, inner_bottleneck_rows, inner_convolved = residual_block_forward(
        activations, inner_squeeze_weight, inner_filter_taps, inner_expand_weight, inner_pair
    )
    final_output, outer_bottleneck_rows, outer_convolved = residual_block_forward(
        outer_block_input, outer_squeeze_weight, outer_filter_taps, outer_expand_weight, outer_pair
    )
    normal_final, factor_final = norm_rows(final_output.astype(jnp.float32))
    normed = normal_final.astype(jnp.bfloat16)
    logits = product_t(normed, decoder)
    exponent = jnp.exp(logits)
    totals = jnp.sum(exponent, axis=-1, keepdims=True)
    classes = jnp.arange(decoder.shape[0], dtype=jnp.int32)
    onehot = (targets[:, None] == classes[None, :]).astype(jnp.float32)
    token_loss = jnp.log(totals[:, 0]) - jnp.sum(logits * onehot, axis=-1)
    dlogits = (32.0 * (exponent / totals - onehot)).astype(jnp.bfloat16)
    gradient_result = norm_back(normal_final, factor_final, product(dlogits, decoder))
    gradient_result = residual_block_backward(
        outer_block_input,
        outer_bottleneck_rows,
        outer_convolved,
        outer_squeeze_weight,
        outer_filter_taps,
        outer_expand_weight,
        outer_pair,
        gradient_result,
    )
    gradient_result = residual_block_backward(
        activations,
        inner_bottleneck_rows,
        inner_convolved,
        inner_squeeze_weight,
        inner_filter_taps,
        inner_expand_weight,
        inner_pair,
        gradient_result,
    )
    return (gradient_result.astype(jnp.bfloat16), token_loss)


BF = jnp.bfloat16
F32 = jnp.float32
ROOT_HALF = math.sqrt(0.5)
BELL = math.sqrt(2.0 / math.pi)


def scaled_norm(values, scale):
    average = jnp.mean(values, axis=-1, keepdims=True)
    centred = values - average
    factor = lax.rsqrt(jnp.mean(centred * centred, axis=-1, keepdims=True) + eps)
    return (centred * (factor * scale), factor)


def activate(values, kept, rows):
    scaled_ref, slope_ref, factor_ref = kept
    scaled, factor = scaled_norm(values, ROOT_HALF)
    half = ROOT_HALF * lax.erf(scaled) + ROOT_HALF
    scaled_ref[rows, :] = scaled
    slope_ref[rows, :] = half + scaled * (BELL * jnp.exp(-(scaled * scaled)))
    factor_ref[rows, :] = jnp.broadcast_to(factor, (factor.shape[0], LANES))
    return (scaled * half).astype(BF)


def back(upward, kept, rows):
    scaled_ref, slope_ref, factor_ref = kept
    scaled = scaled_ref[rows, :]
    through = slope_ref[rows, :] * upward
    mean = jnp.mean(through, axis=-1, keepdims=True)
    along = 2.0 * jnp.mean(through * scaled, axis=-1, keepdims=True)
    return (through - mean - scaled * along) * (factor_ref[rows, :][:, :1] * ROOT_HALF)


def chain_kernel(near, far, block, chunk, last, *refs):
    refs = list(refs)
    first_ref = refs.pop(0)
    x_ref = refs.pop(0) if chunk else first_ref
    before_ref = refs.pop(0) if chunk else None
    *weights_far, dec_ref = refs[:7]
    refs = refs[7:]
    grad_ref = refs.pop(0)
    loss_ref = None if last else refs.pop(0)
    ws_in, wt_in, we_in, ws_out, wt_out, we_out = refs[:6]
    dec_pad, mid_a, mid_b, outer_in, carried = refs[6:11]
    kept = [refs[start : start + 3] for start in range(11, 29, 3)]
    in_a, mid_kept_a, con_a, in_b, mid_kept_b, con_b = kept
    sems = refs[29]
    total, width = x_ref.shape[0], ws_in.shape[0]
    wide, classes = pl.ds(0, width), dec_ref.shape[0]
    starts = range(0, total, block)
    copies = [
        pltpu.make_async_copy(source, target, sems.at[index])
        for index, (source, target) in enumerate(zip(weights_far, refs[:6]))
    ]
    for copy in copies:
        copy.start()

    dec_pad[...] = jnp.zeros_like(dec_pad)
    dec_pad[pl.ds(0, classes), :] = dec_ref[...]

    def wrap(ref):
        ref[pl.ds(0, near), :] = ref[pl.ds(total, near), :]
        ref[pl.ds(total + near, near), :] = ref[pl.ds(near, near), :]

    def near_rows(ref, start, shift):
        return ref[pl.ds(start + near + shift, block), :]

    def far_rows(ref, start, shift):
        at = (start + shift) % total
        if at + block <= total:
            return ref[pl.ds(at, block), :]
        return jnp.concatenate([ref[at:total, :], ref[: at + block - total, :]])

    def conv(behind, here, ahead, taps):
        return product(
            jnp.concatenate([behind, here, ahead], axis=1), taps[...].reshape(-1, taps.shape[2])
        )

    meet = 2 * far % total == 0

    def both_ends(taps):
        return (taps[0].astype(F32) + taps[2].astype(F32)).astype(BF)

    def far_conv(behind, here, ahead, taps):
        if not meet:
            return conv(behind, here, ahead, taps)
        weight = jnp.concatenate([both_ends(taps), taps[1]])
        return product(jnp.concatenate([behind, here], axis=1), weight)

    def far_conv_back(behind, here, ahead, taps):
        if not meet:
            return conv_back(behind, here, ahead, taps)
        weight = jnp.concatenate([both_ends(taps), taps[1]], axis=1)
        return product_t(jnp.concatenate([ahead, here], axis=1), weight)

    def conv_back(behind, here, ahead, taps):
        return product_t(
            jnp.concatenate([ahead, here, behind], axis=1),
            jnp.concatenate([taps[0], taps[1], taps[2]], axis=1),
        )

    for start in starts:
        rows = pl.ds(start, block)
        entry = activate(x_ref[rows, wide].astype(F32), in_a, rows)
        if start == 0:
            copies[0].wait()
        middle = activate(product(entry, ws_in[...]), mid_kept_a, rows)
        mid_a[pl.ds(start + near, block), :] = middle
    wrap(mid_a)

    for copy in copies[1:4]:
        copy.wait()
    for start in starts:
        rows = pl.ds(start, block)
        shifted = [near_rows(mid_a, start, shift) for shift in (-near, 0, near)]
        closing = activate(conv(*shifted, wt_in), con_a, rows)
        following = (x_ref[rows, wide].astype(F32) + product(closing, we_in[...])).astype(BF)
        outer_in[rows, :] = following
        entry = activate(following.astype(F32), in_b, rows)
        mid_b[rows, :] = activate(product(entry, ws_out[...]), mid_kept_b, rows)

    for copy in copies[4:]:
        copy.wait()
    for start in starts:
        rows = pl.ds(start, block)
        shifted = [far_rows(mid_b, start, shift) for shift in (-far, 0, far)]
        closing = activate(far_conv(*shifted, wt_out), con_b, rows)
        final = (outer_in[rows, :].astype(F32) + product(closing, we_out[...])).astype(BF)
        normal, factor = scaled_norm(final.astype(F32), 1.0)
        logits = product_t(normal.astype(BF), dec_pad[...])
        lane = lax.broadcasted_iota(jnp.int32, logits.shape, 1)
        exponent = jnp.where(lane < classes, jnp.exp(logits), 0.0)
        totals = jnp.sum(exponent, axis=-1, keepdims=True)
        target = first_ref[rows, pl.ds(width, LANES)].astype(F32)[:, chunk : chunk + 1]
        onehot = jnp.where(lane.astype(F32) == target, 1.0, 0.0)
        loss = jnp.log(totals) - jnp.sum(logits * onehot, axis=-1, keepdims=True)
        pieces = before_ref[rows, :].astype(F32) if chunk else jnp.zeros_like(logits)
        for part in range(PIECES):
            piece = loss.astype(BF).astype(F32)
            pieces = jnp.where(lane == chunk * PIECES + part, piece, pieces)
            loss = loss - piece
        if last:
            grad_ref[rows, pl.ds(width, LANES)] = pieces.astype(BF)
        else:
            loss_ref[rows, :] = pieces.astype(BF)
        dlogits = (32.0 * (exponent / totals - onehot)).astype(BF)
        upward = norm_back(normal, factor, product(dlogits, dec_pad[...]))
        carried[rows, :] = upward
        dclosing = product_t(upward.astype(BF), we_out[...])
        mid_a[rows, :] = back(dclosing, con_b, rows).astype(BF)

    for start in starts:
        rows = pl.ds(start, block)
        shifted = [far_rows(mid_a, start, shift) for shift in (-far, 0, far)]
        dmiddle = far_conv_back(*shifted, wt_out)
        dsqueezed = back(dmiddle, mid_kept_b, rows).astype(BF)
        upward = carried[rows, :] + back(product_t(dsqueezed, ws_out[...]), in_b, rows)
        carried[rows, :] = upward
        dclosing = product_t(upward.astype(BF), we_in[...])
        mid_b[pl.ds(start + near, block), :] = back(dclosing, con_a, rows).astype(BF)
    wrap(mid_b)

    for start in starts:
        rows = pl.ds(start, block)
        shifted = [near_rows(mid_b, start, shift) for shift in (-near, 0, near)]
        dmiddle = conv_back(*shifted, wt_in)
        dsqueezed = back(dmiddle, mid_kept_a, rows).astype(BF)
        upward = carried[rows, :] + back(product_t(dsqueezed, ws_in[...]), in_a, rows)
        grad_ref[rows, wide] = upward.astype(BF)


VMEM = pl.BlockSpec(memory_space=pltpu.VMEM)
ANY = pl.BlockSpec(memory_space=pl.ANY)


def run_chains(first, rows, before, weights, near, far, block, chunk, last):
    count = first.shape[0]
    width, bottleneck = weights[0].shape
    padded = count + 2 * near
    tile = jax.ShapeDtypeStruct((count, LANES), BF)
    if last:
        out_shape = (jax.ShapeDtypeStruct((count, width + LANES), BF),)
    else:
        out_shape = (jax.ShapeDtypeStruct((count, width), BF), tile)

    def kept(size):
        return [
            pltpu.VMEM((count, size), F32),
            pltpu.VMEM((count, size), F32),
            pltpu.VMEM((count, LANES), F32),
        ]

    one_block = kept(width) + kept(bottleneck) + kept(bottleneck)
    operands = ((first, rows, before) if chunk else (first,)) + weights
    return pl.pallas_call(
        functools.partial(chain_kernel, near, far, block, chunk, last),
        out_shape=out_shape,
        in_specs=[VMEM] * (3 if chunk else 1) + [ANY] * 6 + [VMEM],
        out_specs=(VMEM,) * len(out_shape),
        scratch_shapes=[pltpu.VMEM(weight.shape, BF) for weight in weights[:6]]
        + [
            pltpu.VMEM((LANES, width), BF),
            pltpu.VMEM((padded, bottleneck), BF),
            pltpu.VMEM((padded, bottleneck), BF),
            pltpu.VMEM((count, width), BF),
            pltpu.VMEM((count, width), F32),
        ]
        + one_block
        + one_block
        + [pltpu.SemaphoreType.DMA((6,))],
        compiler_params=pltpu.CompilerParams(vmem_limit_bytes=KERNEL_VMEM),
        cost_estimate=pl.CostEstimate(
            flops=count * 36 * width * bottleneck, bytes_accessed=24 << 20, transcendentals=0
        ),
    )(*operands)


def pack_kernel(chunks, x_ref, target_far, out_ref, target_ref, buffer, in_sems, out_sems):
    target_copy = pltpu.make_async_copy(target_far, target_ref, in_sems.at[PACK_STEPS])
    target_copy.start()
    part, width = buffer.shape[0], x_ref.shape[1]
    size = part // PACK_STEPS
    arrivals, departures = [], []
    for step in range(PACK_STEPS):
        rows = pl.ds(step * size, size)
        here = buffer.at[rows, pl.ds(0, width)]
        arrivals.append(pltpu.make_async_copy(x_ref.at[rows, :], here, in_sems.at[step]))
        departures.append(
            pltpu.make_async_copy(buffer.at[rows, :], out_ref.at[rows, :], out_sems.at[step])
        )
        arrivals[-1].start()
    target_copy.wait()
    lane = lax.broadcasted_iota(jnp.int32, (LANES, LANES), 1)
    for start in range(0, part, LANES):
        tile = jnp.zeros((LANES, LANES), F32)
        for chunk in range(chunks):
            row = target_ref[pl.ds((chunk * part + start) // LANES, 1), :].astype(F32)
            column = jnp.transpose(jnp.broadcast_to(row, (LANES, LANES)))
            tile = jnp.where(lane == chunk, column, tile)
        buffer[pl.ds(start, LANES), pl.ds(width, LANES)] = tile.astype(BF)
    for arrival, departure in zip(arrivals, departures):
        arrival.wait()
        departure.start()
    for departure in departures:
        departure.wait()


def pack(activations, targets, chunks):
    rows, width = activations.shape
    shape = (rows // chunks, width + LANES)
    return pl.pallas_call(
        functools.partial(pack_kernel, chunks),
        out_shape=jax.ShapeDtypeStruct(shape, BF),
        in_specs=[ANY, ANY],
        out_specs=ANY,
        scratch_shapes=[
            pltpu.VMEM((rows // LANES, LANES), targets.dtype),
            pltpu.VMEM(shape, BF),
            pltpu.SemaphoreType.DMA((PACK_STEPS + 1,)),
            pltpu.SemaphoreType.DMA((PACK_STEPS,)),
        ],
        compiler_params=pltpu.CompilerParams(vmem_limit_bytes=WHOLE_VMEM),
    )(activations, targets.reshape(rows // LANES, LANES))


def rest_kernel(x_ref, *refs):
    outs, sems = refs[:-1], refs[-1]
    part = outs[0].shape[0]
    copies = [
        pltpu.make_async_copy(x_ref.at[pl.ds((chunk + 1) * part, part), :], out, sems.at[chunk])
        for chunk, out in enumerate(outs)
    ]
    for copy in copies:
        copy.start()
    for copy in copies:
        copy.wait()


def rest(activations, chunks):
    rows, width = activations.shape
    return pl.pallas_call(
        rest_kernel,
        out_shape=(jax.ShapeDtypeStruct((rows // chunks, width), BF),) * (chunks - 1),
        in_specs=[ANY],
        out_specs=(VMEM,) * (chunks - 1),
        scratch_shapes=[pltpu.SemaphoreType.DMA((chunks - 1,))],
        compiler_params=pltpu.CompilerParams(vmem_limit_bytes=WHOLE_VMEM),
    )(activations)


def unpack_kernel(*refs):
    *pieces, out_ref, loss_far, loss_ref, sems = refs
    part, width = pieces[-1].shape[0], out_ref.shape[1]
    copies = []
    for chunk, piece in enumerate(pieces):
        place = out_ref.at[pl.ds(chunk * part, part), :]
        copies.append(pltpu.make_async_copy(piece.at[:, pl.ds(0, width)], place, sems.at[chunk]))
        copies[-1].start()
    for start in range(0, part, LANES):
        tile = pieces[-1][pl.ds(start, LANES), pl.ds(width, LANES)].astype(F32)
        flat = jnp.transpose(tile)
        for chunk in range(len(pieces)):
            first = chunk * PIECES
            lines = [flat[first + index : first + index + 1] for index in range(PIECES)]
            loss_ref[pl.ds((chunk * part + start) // LANES, 1), :] = sum(lines[1:], lines[0])
    copies.append(pltpu.make_async_copy(loss_ref, loss_far, sems.at[len(pieces)]))
    copies[-1].start()
    for copy in copies:
        copy.wait()


def unpack(homes, width):
    chunks, part = len(homes), homes[0].shape[0]
    rows = chunks * part
    result, losses = pl.pallas_call(
        unpack_kernel,
        out_shape=(
            jax.ShapeDtypeStruct((rows, width), BF),
            jax.ShapeDtypeStruct((rows // LANES, LANES), F32),
        ),
        in_specs=[VMEM] * chunks,
        out_specs=(ANY, ANY),
        scratch_shapes=[
            pltpu.VMEM((rows // LANES, LANES), F32),
            pltpu.SemaphoreType.DMA((chunks + 1,)),
        ],
        compiler_params=pltpu.CompilerParams(vmem_limit_bytes=SMALL_VMEM),
    )(*homes)
    return (result, losses.reshape(rows))


def on_device_chains(chunks, block, activations, targets, *weights):
    axes = ("coarse", "fine")
    devices = lax.axis_size(axes)
    rows, width = activations.shape
    part = rows // chunks
    each = part // devices
    near = FINE_HOP * each
    far = COARSE_HOP * lax.axis_size("fine") * each

    def spread(values):
        shaped = values.reshape((devices, each) + values.shape[1:])
        moved = lax.all_to_all(shaped, axes, 0, 0, tiled=True)
        return moved.reshape(values.shape)

    there = []
    pieces = [pack(activations, targets, chunks)]
    if chunks > 1:
        pieces += rest(activations, chunks)
    for piece in pieces:
        there.append(spread(piece))
    losses = None
    homes = []
    for chunk in range(chunks):
        grad, *losses = run_chains(
            there[0], there[chunk], *(losses or [None]), weights, near, far, block, chunk,
            chunk == chunks - 1,
        )
        homes.append(spread(grad))
    return unpack(homes, width)


def chains_fit(mesh, rows, chunks, block):
    devices = mesh.shape["coarse"] * mesh.shape["fine"]
    part = rows // chunks
    if rows % chunks or part % devices or part % block or part % LANES:
        return False
    each = part // devices
    far = COARSE_HOP * mesh.shape["fine"] * each
    near = FINE_HOP * each
    return near % 16 == 0 and far % 16 == 0 and chunks * PIECES <= LANES


def solution(mesh):
    in_specs = (
        P(("coarse", "fine"), None),
        P(("coarse", "fine")),
        P(),
        P(),
        P(),
        P(),
        P(),
        P(),
        P(),
    )
    out_specs = (P(("coarse", "fine"), None), P(("coarse", "fine")))

    def step(activations, *others):
        rows = activations.shape[0] // mesh.size
        chained = chains_fit(mesh, rows, CHUNKS, BLOCK)
        body = functools.partial(on_device_chains, CHUNKS, BLOCK) if chained else on_device

        spread = jax.shard_map(
            body, mesh=mesh, in_specs=in_specs, out_specs=out_specs, check_vma=False
        )
        return spread(activations, *others)

    return step
```
